512 devices in a mesh: space: 128 (over z, x_hi, y), depth: 4 (over x_lo, core).
Axes of the slice: x: 4 (x_hi: 2, x_lo: 2; x = x_hi * 2 + x_lo), y: 4, z: 16, core: 2. Of those that a mesh axis runs over, the one named last changes fastest.
Arguments:
- features: bfloat16 [128, 4, 512, 128], P('space', 'depth'), may hold values from -6 to 6
- cotangent: bfloat16 [128, 4, 512, 128], P('space', 'depth'), may hold values from -6 to 6
- first_kernel: bfloat16 [27, 128, 128], replicated, may hold values from -0.109375 to 0.109375
- second_kernel: bfloat16 [27, 128, 128], replicated, may hold values from -0.109375 to 0.109375
- slot_tile: int32 [128, 4], P('space'), may hold values from 0 to 3, as said below
- slot_used: int32 [128, 4], P('space'), may hold values from 0 to 1, as said below
Outputs:
- input_grad: bfloat16 [128, 4, 512, 128], P('space', 'depth')
- first_kernel_grad: float32 [442368], P(('space', 'depth'))
- second_kernel_grad: float32 [442368], P(('space', 'depth'))
The draws below stay inside these ranges and needn't reach their ends.
Inputs may be any that keep to these rules, and one draw needn't show every extreme that they name: `slot_tile`: in each column the used slots hold distinct z positions that form one unbroken run; in some column every slot is used. `slot_used`: every column has at least one used slot.
All inputs are finite; a program needn't handle non-finite values.
Results may differ from the reference program's by a relative error of at most 0.006.
Values may be sent and summed in bfloat16 or wider, within the bound.
A program may use at most 64 MiB of HBM per device.

```python
import jax
import jax.numpy as jnp
from jax import lax

C = 128
TE = 8
GY = 8
VOX = 512
ZT = 4
COLUMNS = 128
GX = 16


def column_layout(key):
    base_key = jax.random.fold_in(key, 7)
    sub_keys = jax.random.split(base_key, 4)
    lengths = jax.random.randint(sub_keys[0], (COLUMNS,), 1, ZT + 1)
    forced = jax.random.randint(sub_keys[1], (), 0, COLUMNS)
    lengths = jnp.where(jnp.arange(COLUMNS) == forced, ZT, lengths)
    starts = jax.random.randint(sub_keys[2], (COLUMNS,), 0, ZT + 1 - lengths)

    def column_order(column_key):
        return jax.random.permutation(column_key, ZT)
    ranking = jax.vmap(column_order)(jax.random.split(sub_keys[3], COLUMNS))
    in_use = (ranking < lengths[:, None]).astype(jnp.int32)
    tile_spots = ((starts[:, None] + ranking) % ZT).astype(jnp.int32)
    return (tile_spots, in_use)


def draw_slot_tile(key, part):
    return column_layout(key)[0]


def draw_slot_used(key, part):
    return column_layout(key)[1]


def shard_levels(stream_key, shape, pieces, low, high):
    def one(axis_at, shards_of):
        heights = jax.random.uniform(jax.random.fold_in(jax.random.fold_in(stream_key, 6), axis_at), (shards_of,), jnp.float32, low / len(pieces), high / len(pieces))
        return jnp.repeat(jnp.exp(heights), shape[axis_at] // shards_of).reshape((-1,) + (1,) * (len(shape) - axis_at - 1))

    factor_of = one(*pieces[0])
    for cut in pieces[1:]:
        factor_of = factor_of * one(*cut)
    return factor_of


def normal_values(rng, shape, scale, bound, cuts=(), kind=jnp.bfloat16):
    drawn = scale * jax.random.normal(rng, shape, jnp.float32)
    if cuts:
        drawn = drawn * shard_levels(rng, shape, cuts, -0.22, 0.18)
    return jnp.clip(drawn, -bound, bound).astype(kind)


def setup_inputs(seed: int = 0) -> dict:
    streams_of = jax.random.split(jax.random.key(seed), 7)
    return {
        "features": normal_values(streams_of[0], (COLUMNS, ZT, VOX, C), 1.0, 6.0, ((0, 128), (1, 4))),
        "cotangent": normal_values(streams_of[1], (COLUMNS, ZT, VOX, C), 1.0, 6.0, ((0, 128), (1, 4))),
        "first_kernel": normal_values(streams_of[2], (27, C, C), (27 * C) ** -0.5, 0.109375),
        "second_kernel": normal_values(streams_of[3], (27, C, C), (27 * C) ** -0.5, 0.109375),
        "slot_tile": draw_slot_tile(jax.random.fold_in(streams_of[6], 71), 0),
        "slot_used": draw_slot_used(jax.random.fold_in(streams_of[6], 71), 0),
    }


SLOPE_COEF = 0.7978845608028654
CUBIC_COEF = 0.044715

def gelu_pair(values):
    inner_arg = SLOPE_COEF * (values + CUBIC_COEF * values * values * values)
    tangent = jnp.tanh(inner_arg)
    output = 0.5 * values * (1.0 + tangent)
    derivative = 0.5 * (1.0 + tangent) + 0.5 * values * (1.0 - tangent * tangent) * SLOPE_COEF * (1.0 + 3.0 * CUBIC_COEF * values * values)
    return (output, derivative)

def columns_to_volume(dense):
    width = dense.shape[-1]
    shaped = dense.reshape(GX, GY, ZT, TE, TE, TE, width)
    return jnp.transpose(shaped, (2, 3, 0, 4, 1, 5, 6)).reshape(ZT * TE, GX * TE, GY * TE, width)

def volume_to_columns(volume):
    width = volume.shape[-1]
    shaped = volume.reshape(ZT, TE, GX, TE, GY, TE, width)
    return jnp.transpose(shaped, (2, 4, 0, 1, 3, 5, 6)).reshape(COLUMNS, ZT, VOX, width)

def convolve(volume, kernel):
    weights = kernel.astype(jnp.float32).reshape(3, 3, 3, kernel.shape[1], kernel.shape[2])
    result = lax.conv_general_dilated(volume.astype(jnp.float32)[None], weights, (1, 1, 1), ((1, 1), (1, 1), (1, 1)), dimension_numbers=('NDHWC', 'DHWIO', 'NDHWC'), precision=lax.Precision.HIGHEST)
    return result[0]

def convolve_back(volume, kernel):
    weights = kernel.astype(jnp.float32).reshape(3, 3, 3, kernel.shape[1], kernel.shape[2])
    flipped = jnp.transpose(weights[::-1, ::-1, ::-1], (0, 1, 2, 4, 3))
    result = lax.conv_general_dilated(volume.astype(jnp.float32)[None], flipped, (1, 1, 1), ((1, 1), (1, 1), (1, 1)), dimension_numbers=('NDHWC', 'DHWIO', 'NDHWC'), precision=lax.Precision.HIGHEST)
    return result[0]

def kernel_grad(source, delta):
    padded = jnp.pad(source.astype(jnp.float32), ((1, 1), (1, 1), (1, 1), (0, 0)))
    delta_f = delta.astype(jnp.float32)

    def per_tap(kernel_tap):
        z_step = (kernel_tap // 9).astype(jnp.int32)
        x_step = (kernel_tap // 3 % 3).astype(jnp.int32)
        y_step = (kernel_tap % 3).astype(jnp.int32)
        zero_idx = jnp.zeros((), jnp.int32)
        window = lax.dynamic_slice(padded, (z_step, x_step, y_step, zero_idx), delta_f.shape[:3] + (padded.shape[3],))
        return jnp.einsum('zxyi,zxyo->io', window, delta_f, precision=lax.Precision.HIGHEST)
    summed = lax.map(per_tap, jnp.arange(27).astype(jnp.int32))
    return (summed * (1.0 / VOX)).reshape(-1)

def reference(features, cotangent, first_kernel, second_kernel, slot_tile, slot_used):
    positions = jnp.arange(ZT).astype(jnp.int32)
    placement = ((slot_tile[:, None, :] == positions[None, :, None]) & (slot_used[:, None, :] == 1)).astype(jnp.float32)
    occupancy = lax.optimization_barrier(jnp.sum(placement, axis=2))
    occupied = columns_to_volume(jnp.broadcast_to(occupancy[:, :, None, None], (COLUMNS, ZT, VOX, 1)))
    source = columns_to_volume(jnp.einsum('ctj,cjvk->ctvk', placement, features.astype(jnp.float32))).astype(jnp.bfloat16)
    upstream = columns_to_volume(jnp.einsum('ctj,cjvk->ctvk', placement, cotangent.astype(jnp.float32))).astype(jnp.bfloat16)
    pre_one = convolve(source, first_kernel)
    act_value, slope_one = gelu_pair(pre_one)
    act_one = (act_value * occupied).astype(jnp.bfloat16)
    pre_two = convolve(act_one, second_kernel)
    slope_two = gelu_pair(pre_two)[1]
    delta_two = (upstream.astype(jnp.float32) * slope_two * occupied).astype(jnp.bfloat16)
    delta_one = (convolve_back(delta_two, second_kernel) * slope_one * occupied).astype(jnp.bfloat16)
    back_zero = volume_to_columns(convolve_back(delta_one, first_kernel))
    input_grad = jnp.einsum('ctj,ctvk->cjvk', placement, back_zero).astype(jnp.bfloat16)
    first_kernel_grad = kernel_grad(source, delta_one)
    second_kernel_grad = kernel_grad(act_one, delta_two)
    return (input_grad, first_kernel_grad, second_kernel_grad)
```

```python
import functools

import jax
import jax.numpy as jnp
from jax import lax
from jax.experimental import pallas as pl
from jax.experimental.pallas import tpu as pltpu
from jax.sharding import PartitionSpec as P

MESH = pl.DeviceIdType.MESH

TE = 8
GY = 8


SLOPE_COEF = 0.7978845608028654
CUBIC_COEF = 0.044715


def from_behind(block, axis, distance):
    devices = range(lax.axis_size(axis))
    route = [(i - distance, i) for i in devices if i - distance in devices]
    return lax.ppermute(block, axis, route)


def gelu_pair(values):
    inner_arg = SLOPE_COEF * (values + CUBIC_COEF * values * values * values)
    tangent = jnp.tanh(inner_arg)
    output = 0.5 * values * (1.0 + tangent)
    derivative = 0.5 * (1.0 + tangent) + 0.5 * values * (1.0 - tangent * tangent) * SLOPE_COEF * (
        1.0 + 3.0 * CUBIC_COEF * values * values
    )
    return (output, derivative)


def gelu_slope(values):
    inner_arg = SLOPE_COEF * (values + CUBIC_COEF * values * values * values)
    tangent = jnp.tanh(inner_arg)
    return 0.5 * (1.0 + tangent) + 0.5 * values * (1.0 - tangent * tangent) * SLOPE_COEF * (
        1.0 + 3.0 * CUBIC_COEF * values * values
    )


def place_matrix(slot_tile, slot_used, position_count):
    positions = jnp.arange(position_count, dtype=jnp.int32)
    matches = (slot_tile[0][None, :] == positions[:, None]) & (slot_used[0][None, :] == 1)
    return matches.astype(jnp.bfloat16)


def dense_column(tile_rows, placement):
    summed = jnp.einsum(
        "tj,jvc->tvc",
        placement,
        lax.all_gather(tile_rows, "depth", axis=0, tiled=True),
        preferred_element_type=jnp.float32,
    )
    return summed.astype(jnp.bfloat16).reshape(-1, TE, TE, summed.shape[-1])


def extend_sides(own_block, move_face, space_index):
    y_coord = space_index % GY
    below = move_face(own_block[:, :, -1:, :], 1) * (y_coord > 0).astype(own_block.dtype)
    above = move_face(own_block[:, :, :1, :], -1) * (y_coord < GY - 1).astype(own_block.dtype)
    widened = jnp.concatenate([below, own_block, above], axis=2)
    behind = move_face(widened[:, -1:, :, :], GY)
    ahead = move_face(widened[:, :1, :, :], -GY)
    return jnp.concatenate([behind, widened, ahead], axis=1)


def pad_depth(own_block):
    return jnp.pad(own_block, ((1, 1), (0, 0), (0, 0), (0, 0)))


def windows_at(padded, positions):

    def one_window(z_index):
        return lax.dynamic_slice_in_dim(padded, z_index * TE, TE + 2, 0)

    return jax.vmap(one_window)(positions)


def unfold(windows, flipped):
    pieces = []
    for kernel_tap in range(27):
        z_step, x_step, y_step = (kernel_tap // 9, kernel_tap // 3 % 3, kernel_tap % 3)
        if flipped:
            z_step, x_step, y_step = (2 - z_step, 2 - x_step, 2 - y_step)
        pieces.append(
            windows[:, z_step : z_step + TE, x_step : x_step + TE, y_step : y_step + TE, :]
        )
    stacked = jnp.concatenate(pieces, axis=-1)
    return stacked.reshape(-1, stacked.shape[-1])


def tile_sum(columns, delta):
    return lax.dot_general(
        columns, delta, (((0,), (0,)), ((), ())), preferred_element_type=jnp.float32
    )


PLANE = 16
DEEP = 16
PIECE = 8


def far_first(step, count):
    half = count // 2
    return half + (step + 1) // 2 * (1 - 2 * (step % 2))


class Spot:

    def __init__(self):
        space = lax.axis_index("space")
        self.depth = lax.axis_index("depth")
        self.space = space
        self.z = space // 8
        self.column = space % 8
        self.core = self.depth % 2
        self.x_lo = self.depth // 2
        self.plane = self.column * 2 + self.x_lo

    def plane_peer(self, rank):
        return (self.z * 8 + rank // 2, rank % 2 * 2 + self.core)

    def deep_peer(self, rank):
        return (rank * 8 + self.column, self.depth)

    def column_peer(self, rank):
        return (self.space, rank)


def greet(spot):
    barrier = pltpu.get_barrier_semaphore()

    def tell(peer):
        pl.semaphore_signal(barrier, inc=1, device_id=peer, device_id_type=MESH)

    tell(spot.column_peer(spot.x_lo * 2 + 1 - spot.core))
    tell(spot.column_peer((1 - spot.x_lo) * 2 + 1 - spot.core))

    @pl.loop(0, 15)
    def _(step):
        tell(spot.deep_peer((spot.z + far_first(step, 16)) % 16))

    @pl.loop(0, 15)
    def _(step):
        tell(spot.plane_peer((spot.plane + step + 1) % 16))

    pl.semaphore_wait(barrier, 32)


def send(source, target, send_sem, recv_sem, peer):
    return pltpu.make_async_remote_copy(
        src_ref=source, dst_ref=target, send_sem=send_sem, recv_sem=recv_sem, device_id=peer, device_id_type=MESH
    )


class Scatter:

    def __init__(self, spot, refs):
        self.spot = spot
        (self.halves, self.partner, self.merged, self.plane_in, self.deep_out, self.deep_in, self.pieces, self.sems,
         self.plane_sems, self.deep_sems, self.piece_sems) = refs

    @staticmethod
    def scratch():
        return [
            pltpu.VMEM((2, PLANE, DEEP, PIECE, 128), jnp.bfloat16),
            pltpu.VMEM((PLANE, DEEP, PIECE, 128), jnp.bfloat16),
            pltpu.VMEM((PLANE, DEEP, PIECE, 128), jnp.bfloat16),
            pltpu.VMEM((PLANE, DEEP, PIECE, 128), jnp.bfloat16),
            pltpu.VMEM((DEEP, PIECE, 128), jnp.float32),
            pltpu.VMEM((DEEP, PIECE, 128), jnp.float32),
            pltpu.VMEM((4, PIECE, 128), jnp.float32),
            pltpu.SemaphoreType.DMA((2,)),
            pltpu.SemaphoreType.DMA((2, 16)),
            pltpu.SemaphoreType.DMA((2, 16)),
            pltpu.SemaphoreType.DMA((2, 4)),
        ]

    def cut(self, grad_ref):

        @pl.loop(0, DEEP)
        def _(z):
            rows = grad_ref[pl.ds(pl.multiple_of(z * 216, 8), 216), :]
            rows = jnp.concatenate([rows, jnp.zeros((8, 128), jnp.float32)], axis=0)
            for column in range(8):
                for part in range(4):
                    first = column * 27 + part * 8
                    self.halves[part % 2, column * 2 + part // 2, z] = rows[first : first + 8].astype(jnp.bfloat16)

    def pair_copy(self):
        spot = self.spot
        other = 1 - spot.core
        return send(self.halves.at[other], self.partner, self.sems.at[0], self.sems.at[1],
                    spot.column_peer(spot.x_lo * 2 + other))

    def merge(self):
        core = self.spot.core

        @pl.loop(0, PLANE)
        def _(rank):
            both = self.halves[core, rank].astype(jnp.float32) + self.partner[rank].astype(jnp.float32)
            self.merged[rank] = both.astype(jnp.bfloat16)

    def plane_copy(self, step):
        me = self.spot.plane
        rank = (me + step) % PLANE
        return send(self.merged.at[rank], self.plane_in.at[me], self.plane_sems.at[0, rank], self.plane_sems.at[1, me],
                    self.spot.plane_peer(rank))

    def plane_arrival(self, step):
        me = self.spot.plane
        rank = (me + step) % PLANE
        return send(self.merged.at[rank], self.plane_in.at[rank], self.plane_sems.at[0, rank],
                    self.plane_sems.at[1, rank], self.spot.plane_peer(rank))

    def plane_start(self):

        @pl.loop(1, PLANE)
        def _(step):
            self.plane_copy(step).start()

    def plane_finish(self):
        me = self.spot.plane
        self.plane_in[me] = self.merged[me]

        @pl.loop(1, PLANE)
        def _(step):
            self.plane_arrival(step).wait_recv()

        @pl.loop(0, DEEP)
        def _(z):
            total = jnp.zeros((PIECE, 128), jnp.float32)
            for rank in range(PLANE):
                total = total + self.plane_in[rank, z].astype(jnp.float32)
            self.deep_out[z] = total

    def deep_copy(self, step):
        me = self.spot.z
        rank = (me + far_first(step, DEEP)) % DEEP
        return send(self.deep_out.at[rank], self.deep_in.at[me], self.deep_sems.at[0, rank], self.deep_sems.at[1, me],
                    self.spot.deep_peer(rank))

    def deep_arrival(self, step):
        me = self.spot.z
        rank = (me + far_first(step, DEEP)) % DEEP
        return send(self.deep_out.at[rank], self.deep_in.at[rank], self.deep_sems.at[0, rank],
                    self.deep_sems.at[1, rank], self.spot.deep_peer(rank))

    def deep_start(self):

        @pl.loop(0, DEEP - 1)
        def _(step):
            self.deep_copy(step).start()

    def deep_finish(self):
        me = self.spot.z
        self.deep_in[me] = self.deep_out[me]

        @pl.loop(0, DEEP - 1)
        def _(step):
            self.deep_arrival(step).wait_recv()

        total = jnp.zeros((PIECE, 128), jnp.float32)
        for rank in range(DEEP):
            total = total + self.deep_in[rank]
        self.pieces[self.spot.depth] = total * (1.0 / 512)

    def piece_copy(self, step):
        me = self.spot.depth
        rank = (me + step) % 4
        return send(self.pieces.at[me], self.pieces.at[me], self.piece_sems.at[0, rank], self.piece_sems.at[1, me],
                    self.spot.column_peer(rank))

    def piece_arrival(self, step):
        me = self.spot.depth
        rank = (me + step) % 4
        return send(self.pieces.at[rank], self.pieces.at[rank], self.piece_sems.at[0, rank],
                    self.piece_sems.at[1, rank], self.spot.column_peer(rank))

    def piece_start(self):
        for step in range(1, 4):
            self.piece_copy(step).start()

    def piece_finish(self, out_ref):
        for step in range(1, 4):
            self.piece_arrival(step).wait_recv()
        for rank in range(4):
            out_ref[rank] = self.pieces[rank]

    def drain(self):
        self.pair_copy().wait_send()

        @pl.loop(1, PLANE)
        def _(step):
            self.plane_copy(step).wait_send()

        @pl.loop(0, DEEP - 1)
        def _(step):
            self.deep_copy(step).wait_send()

        for step in range(1, 4):
            self.piece_copy(step).wait_send()


def scatter_kernel(one_ref, two_ref, out_one, out_two, *scratch):
    spot = Spot()
    count = len(scratch) // 2
    pair = [(Scatter(spot, scratch[count:]), two_ref, out_two), (Scatter(spot, scratch[:count]), one_ref, out_one)]
    greet(spot)
    for scatter, grad, _ in pair:
        scatter.cut(grad)
        scatter.pair_copy().start()
    for scatter, _, _ in pair:
        scatter.pair_copy().wait_recv()
        scatter.merge()
        scatter.plane_start()
    for scatter, _, _ in pair:
        scatter.plane_finish()
        scatter.deep_start()
    for scatter, _, _ in pair:
        scatter.deep_finish()
        scatter.piece_start()
    for scatter, _, out in pair:
        scatter.piece_finish(out)
    for scatter, _, _ in pair:
        scatter.drain()


def scatter_both(one, two):
    shape = jax.ShapeDtypeStruct((4, PIECE, 128), jnp.float32)
    return pl.pallas_call(
        scatter_kernel,
        out_shape=(shape, shape),
        in_specs=[pl.BlockSpec(memory_space=pltpu.VMEM)] * 2,
        out_specs=(pl.BlockSpec(memory_space=pltpu.VMEM),) * 2,
        scratch_shapes=Scatter.scratch() * 2,
        compiler_params=pltpu.CompilerParams(collective_id=0, has_side_effects=True, vmem_limit_bytes=40 << 20),
    )(one, two)


def on_device(features, cotangent, first_kernel, second_kernel, slot_tile, slot_used):
    depth_index = lax.axis_index("depth")
    space_index = lax.axis_index("space")
    slot_count = features.shape[1]
    voxels = features.shape[2]
    channels = features.shape[3]
    position_count = slot_tile.shape[1]
    placement = place_matrix(slot_tile, slot_used, position_count)
    own_first = depth_index * slot_count
    own_tiles = lax.dynamic_slice_in_dim(slot_tile[0], own_first, slot_count, 0)
    own_used = lax.dynamic_slice_in_dim(slot_used[0], own_first, slot_count, 0).astype(jnp.float32)
    feature_slots = features[0]
    upstream_slots = cotangent[0]

    def column_move(face, offset):
        return from_behind(face, "space", offset)

    def halo_of(tile_rows):
        column = dense_column(tile_rows.reshape(slot_count, voxels, channels), placement)
        return pad_depth(extend_sides(column, column_move, space_index))

    upstream = upstream_slots.reshape(-1, channels)
    source_column = halo_of(feature_slots)
    alive_rows = jnp.repeat(own_used, voxels)[:, None]
    forward_one = first_kernel.reshape(-1, channels)
    forward_two = second_kernel.reshape(-1, channels)
    backward_one = jnp.transpose(first_kernel, (0, 2, 1)).reshape(-1, channels)
    backward_two = jnp.transpose(second_kernel, (0, 2, 1)).reshape(-1, channels)
    source_cols = unfold(windows_at(source_column, own_tiles), False)
    pre_one = jnp.dot(source_cols, forward_one, preferred_element_type=jnp.float32)
    act_value, slope_one = gelu_pair(pre_one)
    act_one = (act_value * alive_rows).astype(jnp.bfloat16)
    act_cols = unfold(windows_at(halo_of(act_one), own_tiles), False)
    pre_two = jnp.dot(act_cols, forward_two, preferred_element_type=jnp.float32)
    slope_two = gelu_slope(pre_two)
    delta_two = (upstream.astype(jnp.float32) * slope_two * alive_rows).astype(jnp.bfloat16)
    second_grad = tile_sum(act_cols, delta_two)
    back_one = jnp.dot(
        unfold(windows_at(halo_of(delta_two), own_tiles), True),
        backward_two,
        preferred_element_type=jnp.float32,
    )
    delta_one = (back_one * slope_one * alive_rows).astype(jnp.bfloat16)
    first_grad = tile_sum(source_cols, delta_one)
    back_zero = jnp.dot(
        unfold(windows_at(halo_of(delta_one), own_tiles), True),
        backward_one,
        preferred_element_type=jnp.float32,
    )
    used_rows = jnp.repeat(own_used, voxels)[:, None]
    input_grad = (back_zero * used_rows).astype(jnp.bfloat16).reshape(features.shape)
    first_sum, second_sum = scatter_both(first_grad, second_grad)
    own_share = 27 * channels // 4

    def share(total):
        return lax.dynamic_slice_in_dim(total.reshape(-1), depth_index * own_share, own_share, 0)

    first_share, second_share = (share(first_sum), share(second_sum))
    return (input_grad, first_share, second_share)


def solution(mesh):
    return jax.shard_map(
        on_device,
        mesh=mesh,
        in_specs=(
            P("space", "depth", None, None),
            P("space", "depth", None, None),
            P(),
            P(),
            P("space", None),
            P("space", None),
        ),
        out_specs=(P("space", "depth", None, None), P(("space", "depth")), P(("space", "depth"))),
        check_vma=False,
    )
```

```python
import itertools

import jax
import jax.numpy as jnp
from jax import lax
from jax.experimental import pallas as pl
from jax.experimental.pallas import tpu as pltpu
from jax.sharding import PartitionSpec as P

MESH = pl.DeviceIdType.MESH
SLOPE_COEF = 0.7978845608028654
CUBIC_COEF = 0.044715
PLANE = 16
DEEP = 16
PIECE = 8
ROWS = 27 * 128
STEPS = [d for d in itertools.product((-1, 0, 1), repeat=3) if d != (0, 0, 0)]
F32 = jnp.float32
BF16 = jnp.bfloat16


def far_first(step, count):
    half = count // 2
    return half + (step + 1) // 2 * (1 - 2 * (step % 2))


def gelu_terms(values):
    inner = SLOPE_COEF * (values + CUBIC_COEF * values * values * values)
    tangent = jnp.tanh(inner)
    slope = 0.5 * (1.0 + tangent) + 0.5 * values * (1.0 - tangent * tangent) * SLOPE_COEF * (
        1.0 + 3.0 * CUBIC_COEF * values * values
    )
    return 0.5 * values * (1.0 + tangent), slope


class Spot:
    def __init__(self):
        self.space = lax.axis_index("space")
        self.depth = lax.axis_index("depth")
        self.deep = self.space // 8
        self.column = self.space % 8
        self.core = self.depth % 2
        self.x_lo = self.depth // 2
        self.plane = self.column * 2 + self.x_lo

    def plane_peer(self, rank):
        return (self.deep * 8 + rank // 2, rank % 2 * 2 + self.core)

    def deep_peer(self, rank):
        return (rank * 8 + self.column, self.depth)

    def column_peer(self, rank):
        return (self.space, rank)

    def tile_peer(self, step):
        z, x, y = step
        return ((self.deep + x + 16) % 16 * 8 + (self.column + y + 8) % 8, (self.depth + z + 4) % 4)


def greet(spot):
    barrier = pltpu.get_barrier_semaphore()

    def tell(peer):
        pl.semaphore_signal(barrier, inc=1, device_id=peer, device_id_type=MESH)

    @pl.loop(0, 15)
    def _(step):
        tell(spot.deep_peer((spot.deep + far_first(step, 16)) % 16))

    @pl.loop(0, 15)
    def _(step):
        tell(spot.plane_peer((spot.plane + step + 1) % 16))

    for step in STEPS:
        tell(spot.tile_peer(step))
    for step in range(1, 4):
        tell(spot.column_peer((spot.depth + step) % 4))
    pl.semaphore_wait(barrier, 30 + len(STEPS) + 3)


def send(source, target, send_sem, recv_sem, peer):
    return pltpu.make_async_remote_copy(
        src_ref=source, dst_ref=target, send_sem=send_sem, recv_sem=recv_sem, device_id=peer, device_id_type=MESH
    )


class Gather:
    def __init__(self, spot, refs):
        self.spot = spot
        self.tiles, self.sems = refs

    @staticmethod
    def scratch():
        return [pltpu.VMEM((4, 512, 128), BF16), pltpu.SemaphoreType.DMA((2, 4))]

    def copy(self, source, step):
        me = self.spot.depth
        rank = (me + step) % 4
        return send(source, self.tiles.at[me], self.sems.at[0, rank], self.sems.at[1, me], self.spot.column_peer(rank))

    def start(self, source):
        for step in (2, 3, 1):
            self.copy(source, step).start()

    def finish(self, source):
        me = self.spot.depth
        for step in (1, 2, 3):
            rank = (me + step) % 4
            send(source, self.tiles.at[rank], self.sems.at[0, rank], self.sems.at[1, rank],
                 self.spot.column_peer(rank)).wait_recv()

    def drain(self, source):
        for step in (1, 2, 3):
            self.copy(source, step).wait_send()

    def pick(self, weights, rows):
        total = weights[0] * self.tiles[0, rows, :].astype(F32)
        for rank in range(1, 4):
            total = total + weights[rank] * self.tiles[rank, rows, :].astype(F32)
        return total


def side(step):
    return 0 if step == 1 else 1


def last(step):
    return 7 if step == 1 else 0


class Halo:
    def __init__(self, spot, refs):
        self.spot = spot
        (self.tile, self.y_face, self.xy_edge, self.in_z, self.in_x, self.in_y, self.in_zx, self.in_zy, self.in_xy,
         self.in_zxy, self.sems) = refs

    @staticmethod
    def scratch():
        shapes = [(8, 8), (2, 8), (2, 2), (2, 8), (2, 8), (2, 8), (2, 2), (2, 2), (2, 2), (2, 2, 2)]
        return [pltpu.VMEM((*shape, 8, 128), BF16) for shape in shapes] + [pltpu.SemaphoreType.DMA((2, 26))]

    def ends(self, step):
        z, x, y = step
        if y == 0:
            if x == 0:
                return self.tile.at[last(z)], self.in_z.at[side(z)]
            if z == 0:
                return self.tile.at[:, last(x)], self.in_x.at[side(x)]
            return self.tile.at[last(z), last(x)], self.in_zx.at[side(z), side(x)]
        if x == 0:
            if z == 0:
                return self.y_face.at[side(y)], self.in_y.at[side(y)]
            return self.y_face.at[side(y), last(z)], self.in_zy.at[side(z), side(y)]
        if z == 0:
            return self.xy_edge.at[side(x), side(y)], self.in_xy.at[side(x), side(y)]
        return self.xy_edge.at[side(x), side(y)], self.in_zxy.at[side(z), side(x), side(y)]

    def copies(self):
        order = sorted(range(26), key=lambda n: -abs(STEPS[n][2]) * 10 - sum(abs(d) for d in STEPS[n]))
        for n in order:
            source, target = self.ends(STEPS[n])
            yield send(source, target, self.sems.at[0, n], self.sems.at[1, n], self.spot.tile_peer(STEPS[n]))

    def put(self, centre, values):
        rounded = values.astype(BF16).reshape(8, 8, 8, 128)
        self.tile[...] = rounded
        centre[1:9, 1:9] = rounded.astype(F32)
        flat = centre.reshape(800, 128)
        for z in range(8):
            for y in range(2):
                first = ((z + 1) * 10 + 1) * 8 + 7 - 7 * y
                self.y_face[y, z] = flat[pl.ds(first, 8, stride=8), :].astype(BF16)
        for x in range(2):
            for y in range(2):
                first = (10 + 8 - 7 * x) * 8 + 7 - 7 * y
                self.xy_edge[x, y] = flat[pl.ds(first, 8, stride=80), :].astype(BF16)

    def start(self):
        for copy in self.copies():
            copy.start()

    def finish(self, centre, lines, masks, cols):
        for copy in self.copies():
            copy.wait_recv()
        on_z, on_x, on_y = masks
        ends = (0, 9)
        for s in range(2):
            centre[ends[s], 1:9] = self.in_z[s].astype(F32) * on_z[s]
            centre[1:9, ends[s]] = self.in_x[s].astype(F32) * on_x[s]
            lines[s, 1:9, 0:8] = self.in_y[s].astype(F32) * on_y[s]
            for r in range(2):
                centre[ends[s], ends[r]] = self.in_zx[s, r].astype(F32) * (on_z[s] * on_x[r])
                lines[r, ends[s], 0:8] = self.in_zy[s, r].astype(F32) * (on_z[s] * on_y[r])
                rows = self.in_xy[s, r].astype(F32) * (on_x[s] * on_y[r])
                for z in range(8):
                    lines[r, 1 + z, 8 + s : 9 + s] = rows[z : z + 1]
                for q in range(2):
                    rows = self.in_zxy[s, r, q].astype(F32) * (on_z[s] * on_x[r] * on_y[q])
                    row = 7 - 7 * s
                    lines[q, ends[s], 8 + r : 9 + r] = rows[row : row + 1]
        row_id = lax.broadcasted_iota(jnp.int32, (8, 128), 0)

        @pl.loop(0, 10)
        def _(z):
            runs = ([], [], [])
            for x in range(10):
                place = 8 if x == 0 else 9 if x == 9 else x - 1
                middle = centre[z, x]
                low = jnp.broadcast_to(lines[0, z, place : place + 1], (8, 128))
                high = jnp.broadcast_to(lines[1, z, place : place + 1], (8, 128))
                runs[0].append(jnp.where(row_id == 0, low, pltpu.roll(middle, 1, 0)))
                runs[1].append(middle)
                runs[2].append(jnp.where(row_id == 7, high, pltpu.roll(middle, 7, 0)))
            for x in range(3):
                for y in range(3):
                    block = jnp.concatenate(runs[y][x : x + 8], axis=0).astype(BF16)
                    cols[z, :, (3 * x + y) * 128 : (3 * x + y + 1) * 128] = block

    def drain(self):
        for copy in self.copies():
            copy.wait_send()


class Scatter:
    def __init__(self, spot, refs):
        self.spot = spot
        (self.halves, self.partner, self.merged, self.plane_in, self.deep_out, self.deep_in, self.pieces, self.sems,
         self.plane_sems, self.deep_sems, self.piece_sems) = refs

    @staticmethod
    def scratch():
        return [
            pltpu.VMEM((2, PLANE, DEEP, PIECE, 128), BF16),
            pltpu.VMEM((PLANE, DEEP, PIECE, 128), BF16),
            pltpu.VMEM((PLANE, DEEP, PIECE, 128), BF16),
            pltpu.VMEM((PLANE, DEEP, PIECE, 128), BF16),
            pltpu.VMEM((DEEP, PIECE, 128), F32),
            pltpu.VMEM((DEEP, PIECE, 128), F32),
            pltpu.VMEM((4, PIECE, 128), F32),
            pltpu.SemaphoreType.DMA((2,)),
            pltpu.SemaphoreType.DMA((2, 16)),
            pltpu.SemaphoreType.DMA((2, 16)),
            pltpu.SemaphoreType.DMA((2, 4)),
        ]

    def cut(self, grad_ref):

        @pl.loop(0, DEEP)
        def _(z):
            rows = grad_ref[pl.ds(pl.multiple_of(z * 216, 8), 216), :]
            rows = jnp.concatenate([rows, jnp.zeros((8, 128), F32)], axis=0)
            for column in range(8):
                for part in range(4):
                    first = column * 27 + part * 8
                    self.halves[part % 2, column * 2 + part // 2, z] = rows[first : first + 8].astype(BF16)

    def pair_copy(self):
        spot = self.spot
        other = 1 - spot.core
        return send(self.halves.at[other], self.partner, self.sems.at[0], self.sems.at[1],
                    spot.column_peer(spot.x_lo * 2 + other))

    def merge(self):
        self.pair_copy().wait_recv()
        core = self.spot.core

        @pl.loop(0, PLANE)
        def _(rank):
            both = self.halves[core, rank].astype(F32) + self.partner[rank].astype(F32)
            self.merged[rank] = both.astype(BF16)

        @pl.loop(1, PLANE)
        def _(step):
            self.plane_copy(step).start()

    def plane_copy(self, step):
        me = self.spot.plane
        rank = (me + step) % PLANE
        return send(self.merged.at[rank], self.plane_in.at[me], self.plane_sems.at[0, rank], self.plane_sems.at[1, me],
                    self.spot.plane_peer(rank))

    def plane_arrival(self, step):
        me = self.spot.plane
        rank = (me + step) % PLANE
        return send(self.merged.at[rank], self.plane_in.at[rank], self.plane_sems.at[0, rank],
                    self.plane_sems.at[1, rank], self.spot.plane_peer(rank))

    def plane_finish(self):
        me = self.spot.plane
        self.plane_in[me] = self.merged[me]

        @pl.loop(1, PLANE)
        def _(step):
            self.plane_arrival(step).wait_recv()

        @pl.loop(0, DEEP)
        def _(z):
            total = jnp.zeros((PIECE, 128), F32)
            for rank in range(PLANE):
                total = total + self.plane_in[rank, z].astype(F32)
            self.deep_out[z] = total

        @pl.loop(0, DEEP - 1)
        def _(step):
            self.deep_copy(step).start()

    def deep_copy(self, step):
        me = self.spot.deep
        rank = (me + far_first(step, DEEP)) % DEEP
        return send(self.deep_out.at[rank], self.deep_in.at[me], self.deep_sems.at[0, rank], self.deep_sems.at[1, me],
                    self.spot.deep_peer(rank))

    def deep_arrival(self, step):
        me = self.spot.deep
        rank = (me + far_first(step, DEEP)) % DEEP
        return send(self.deep_out.at[rank], self.deep_in.at[rank], self.deep_sems.at[0, rank],
                    self.deep_sems.at[1, rank], self.spot.deep_peer(rank))

    def deep_finish(self):
        me = self.spot.deep
        self.deep_in[me] = self.deep_out[me]

        @pl.loop(0, DEEP - 1)
        def _(step):
            self.deep_arrival(step).wait_recv()

        total = jnp.zeros((PIECE, 128), F32)
        for rank in range(DEEP):
            total = total + self.deep_in[rank]
        self.pieces[self.spot.depth] = total * (1.0 / 512)
        for step in range(1, 4):
            self.piece_copy(step).start()

    def piece_copy(self, step):
        me = self.spot.depth
        rank = (me + step) % 4
        return send(self.pieces.at[me], self.pieces.at[me], self.piece_sems.at[0, rank], self.piece_sems.at[1, me],
                    self.spot.column_peer(rank))

    def piece_arrival(self, step):
        me = self.spot.depth
        rank = (me + step) % 4
        return send(self.pieces.at[rank], self.pieces.at[rank], self.piece_sems.at[0, rank],
                    self.piece_sems.at[1, rank], self.spot.column_peer(rank))

    def piece_finish(self, out_ref):
        for step in range(1, 4):
            self.piece_arrival(step).wait_recv()
        for rank in range(4):
            out_ref[rank] = self.pieces[rank]

    def drain(self):
        self.pair_copy().wait_send()

        @pl.loop(1, PLANE)
        def _(step):
            self.plane_copy(step).wait_send()

        @pl.loop(0, DEEP - 1)
        def _(step):
            self.deep_copy(step).wait_send()

        for step in range(1, 4):
            self.piece_copy(step).wait_send()


def convolve(cols, kernel_ref):
    total = None
    for z in range(3):
        rows = cols[z : z + 8].reshape(512, 9 * 128)
        term = jnp.dot(rows, kernel_ref[z], preferred_element_type=F32)
        total = term if total is None else total + term
    return total


def turn(kernel_ref, turned):
    @pl.loop(0, 27)
    def _(k):
        turned[26 - k] = kernel_ref[k].T


def kernel_gradient(cols, delta, grad_ref):
    for z in range(3):
        rows = cols[z : z + 8].reshape(512, 9 * 128)
        grad_ref[z * 1152 : (z + 1) * 1152] = lax.dot_general(
            rows, delta, (((0,), (0,)), ((), ())), preferred_element_type=F32
        )


def body(features, cotangent, first_hbm, second_hbm, slot_tile, slot_used, grad_out, first_out, second_out, *scratch):
    spot = Spot()
    scratch = list(scratch)

    def take(kind):
        count = len(kind.scratch())
        refs = scratch[:count]
        del scratch[:count]
        return kind(spot, refs)

    source_in, upstream_in, back_in = (take(Gather) for _ in range(3))
    halo_one, halo_two, halo_three, halo_four = (take(Halo) for _ in range(4))
    scatter_one, scatter_two = (take(Scatter) for _ in range(2))
    (first_kernel, second_kernel, first_turned, second_turned, centre, lines, source_cols, act_cols, delta_cols, grad_one,
     grad_two, upstream, slope_one, result, load_sems) = scratch

    loads = [
        pltpu.make_async_copy(first_hbm, first_kernel, load_sems.at[0]),
        pltpu.make_async_copy(second_hbm, second_kernel, load_sems.at[1]),
    ]
    for load in loads:
        load.start()
    greet(spot)
    source_in.start(features)
    upstream_in.start(cotangent)

    me = spot.depth
    source_in.tiles[me] = features[...]
    upstream_in.tiles[me] = cotangent[...]
    weights = [jnp.where(slot_tile[0, j] == me, 1.0, 0.0) * slot_used[0, j].astype(F32) for j in range(4)]
    alive = weights[0] + weights[1] + weights[2] + weights[3]
    own_tile = slot_tile[0, me]
    own_used = slot_used[0, me].astype(F32)

    def mask(condition):
        return jnp.where(condition, 1.0, 0.0)

    masks = (
        (mask(spot.depth > 0), mask(spot.depth < 3)),
        (mask(spot.deep > 0), mask(spot.deep < 15)),
        (mask(spot.column > 0), mask(spot.column < 7)),
    )
    for load in loads:
        load.wait()
    turn(second_kernel, second_turned)
    turn(first_kernel, first_turned)
    first_taps = first_kernel.reshape(3, 1152, 128)
    second_taps = second_kernel.reshape(3, 1152, 128)
    first_back = first_turned.reshape(3, 1152, 128)
    second_back = second_turned.reshape(3, 1152, 128)

    source_in.finish(features)
    halo_one.put(centre, source_in.pick(weights, slice(None)))
    halo_one.start()
    upstream_in.finish(cotangent)
    upstream[...] = upstream_in.pick(weights, slice(None))
    halo_one.finish(centre, lines, masks, source_cols)
    act, slope = gelu_terms(convolve(source_cols, first_taps))
    slope_one[...] = slope * alive
    halo_two.put(centre, act * alive)
    halo_two.start()
    halo_two.finish(centre, lines, masks, act_cols)
    _, slope = gelu_terms(convolve(act_cols, second_taps))
    halo_three.put(centre, upstream[...] * slope * alive)
    halo_three.start()
    kernel_gradient(act_cols, halo_three.tile[...].reshape(512, 128), grad_two)
    scatter_two.cut(grad_two)
    scatter_two.pair_copy().start()
    halo_three.finish(centre, lines, masks, delta_cols)
    halo_four.put(centre, convolve(delta_cols, second_back) * slope_one[...])
    halo_four.start()
    kernel_gradient(source_cols, halo_four.tile[...].reshape(512, 128), grad_one)
    scatter_one.cut(grad_one)
    scatter_one.pair_copy().start()
    scatter_two.merge()
    scatter_one.merge()
    halo_four.finish(centre, lines, masks, delta_cols)
    result[...] = convolve(delta_cols, first_back).astype(BF16)
    back_in.start(result)
    back_in.tiles[me] = result[...]
    scatter_two.plane_finish()
    scatter_one.plane_finish()
    back_in.finish(result)
    picks = [mask(own_tile == t) * own_used for t in range(4)]
    grad_out[...] = back_in.pick(picks, slice(None)).astype(BF16)
    scatter_two.deep_finish()
    scatter_one.deep_finish()
    scatter_two.piece_finish(second_out)
    scatter_one.piece_finish(first_out)
    source_in.drain(features)
    upstream_in.drain(cotangent)
    back_in.drain(result)
    for halo in (halo_one, halo_two, halo_three, halo_four):
        halo.drain()
    scatter_two.drain()
    scatter_one.drain()


def fused(features, cotangent, first_kernel, second_kernel, slot_tile, slot_used):
    whole = pl.BlockSpec(memory_space=pltpu.VMEM)
    left = pl.BlockSpec(memory_space=pl.ANY)
    small = pl.BlockSpec(memory_space=pltpu.SMEM)
    piece = jax.ShapeDtypeStruct((4, PIECE, 128), F32)
    cols = pltpu.VMEM((10, 64, 9 * 128), BF16)
    kernel = pltpu.VMEM((27, 128, 128), BF16)
    scratch = Gather.scratch() * 3 + Halo.scratch() * 4 + Scatter.scratch() * 2
    scratch += [kernel] * 4 + [pltpu.VMEM((10, 10, 8, 128), F32), pltpu.VMEM((2, 10, 16, 128), F32)] + [cols] * 3
    scratch += [pltpu.VMEM((ROWS, 128), F32)] * 2 + [pltpu.VMEM((512, 128), F32)] * 2
    scratch += [pltpu.VMEM((512, 128), BF16), pltpu.SemaphoreType.DMA((2,))]
    return pl.pallas_call(
        body,
        out_shape=(jax.ShapeDtypeStruct((512, 128), BF16), piece, piece),
        in_specs=[whole, whole, left, left, small, small],
        out_specs=(whole, whole, whole),
        scratch_shapes=scratch,
        compiler_params=pltpu.CompilerParams(collective_id=0, has_side_effects=True, vmem_limit_bytes=56 << 20),
    )(features, cotangent, first_kernel, second_kernel, slot_tile, slot_used)


def on_device(features, cotangent, first_kernel, second_kernel, slot_tile, slot_used):
    grad, first_sum, second_sum = fused(
        features.reshape(512, 128), cotangent.reshape(512, 128), first_kernel, second_kernel, slot_tile, slot_used
    )
    own_share = ROWS // 4

    def share(total):
        return lax.dynamic_slice_in_dim(total.reshape(-1), lax.axis_index("depth") * own_share, own_share, 0)

    return (grad.reshape(features.shape), share(first_sum), share(second_sum))


def solution(mesh):
    tiles = P("space", "depth", None, None)
    slots = P("space", None)
    share = P(("space", "depth"))
    return jax.shard_map(
        on_device,
        mesh=mesh,
        in_specs=(tiles, tiles, P(), P(), slots, slots),
        out_specs=(tiles, share, share),
        check_vma=False,
    )
```

```python
import itertools

import jax
import jax.numpy as jnp
from jax import lax
from jax.experimental import pallas as pl
from jax.experimental.pallas import tpu as pltpu
from jax.sharding import PartitionSpec as P

MESH = pl.DeviceIdType.MESH
SLOPE_COEF = 0.7978845608028654
CUBIC_COEF = 0.044715
PLANE = 16
DEEP = 16
PIECE = 8
ROWS = 27 * 128
STEPS = [d for d in itertools.product((-1, 0, 1), repeat=3) if d != (0, 0, 0)]
F32 = jnp.float32
BF16 = jnp.bfloat16


def far_first(step, count):
    half = count // 2
    return half + (step + 1) // 2 * (1 - 2 * (step % 2))


def gelu_terms(values):
    inner = SLOPE_COEF * (values + CUBIC_COEF * values * values * values)
    tangent = jnp.tanh(inner)
    slope = 0.5 * (1.0 + tangent) + 0.5 * values * (1.0 - tangent * tangent) * SLOPE_COEF * (
        1.0 + 3.0 * CUBIC_COEF * values * values
    )
    return 0.5 * values * (1.0 + tangent), slope


class Spot:
    def __init__(self):
        self.space = lax.axis_index("space")
        self.depth = lax.axis_index("depth")
        self.deep = self.space // 8
        self.column = self.space % 8
        self.core = self.depth % 2
        self.x_lo = self.depth // 2
        self.plane = self.column * 2 + self.x_lo

    def plane_peer(self, rank):
        return (self.deep * 8 + rank // 2, rank % 2 * 2 + self.core)

    def deep_peer(self, rank):
        return (rank * 8 + self.column, self.depth)

    def column_peer(self, rank):
        return (self.space, rank)

    def tile_peer(self, step):
        z, x, y = step
        return ((self.deep + x + 16) % 16 * 8 + (self.column + y + 8) % 8, (self.depth + z + 4) % 4)


def greet(spot):
    barrier = pltpu.get_barrier_semaphore()

    def tell(peer):
        pl.semaphore_signal(barrier, inc=1, device_id=peer, device_id_type=MESH)

    for step in STEPS:
        tell(spot.tile_peer(step))
    for step in range(1, 4):
        tell(spot.column_peer((spot.depth + step) % 4))
    pl.semaphore_wait(barrier, len(STEPS) + 3)


class News:
    def __init__(self, spot, refs):
        self.spot = spot
        (self.sem,) = refs

    @staticmethod
    def scratch():
        return [pltpu.SemaphoreType.REGULAR((3,))]

    def peers(self, level):
        reach = 2**level
        steps = [(0, reach, 0), (0, -reach, 0), (0, 0, reach)] + ([(0, 0, -reach)] if level < 2 else [])
        return [self.spot.tile_peer(step) for step in steps]

    def tell(self, level):
        for peer in self.peers(level):
            pl.semaphore_signal(self.sem.at[level], inc=1, device_id=peer, device_id_type=MESH)

    def hear(self, level):
        pl.semaphore_wait(self.sem.at[level], len(self.peers(level)))


def send(source, target, send_sem, recv_sem, peer):
    return pltpu.make_async_remote_copy(
        src_ref=source, dst_ref=target, send_sem=send_sem, recv_sem=recv_sem, device_id=peer, device_id_type=MESH
    )


class Gather:
    def __init__(self, spot, refs):
        self.spot = spot
        self.tiles, self.sems = refs
        self.me = spot.depth
        self.pair = spot.x_lo * 2 + 1 - spot.core
        self.across = (1 - spot.x_lo) * 2 + spot.core
        self.diagonal = (1 - spot.x_lo) * 2 + 1 - spot.core

    @staticmethod
    def scratch():
        return [pltpu.VMEM((4, 512, 128), BF16), pltpu.SemaphoreType.DMA((2, 3))]

    def copy(self, way):
        tile = self.across if way == 2 else self.me
        peer = self.across if way == 0 else self.pair
        return send(self.tiles.at[tile], self.tiles.at[tile], self.sems.at[0, way], self.sems.at[1, way],
                    self.spot.column_peer(peer))

    def arrival(self, way):
        tile = (self.across, self.pair, self.diagonal)[way]
        peer = self.across if way == 0 else self.pair
        return send(self.tiles.at[tile], self.tiles.at[tile], self.sems.at[0, way], self.sems.at[1, way],
                    self.spot.column_peer(peer))

    def start(self):
        self.copy(0).start()
        self.copy(1).start()

    def relay(self):
        self.arrival(0).wait_recv()
        self.copy(2).start()

    def finish(self):
        self.arrival(1).wait_recv()
        self.arrival(2).wait_recv()

    def drain(self):
        for way in range(3):
            self.copy(way).wait_send()

    def pick(self, weights, rows):
        total = weights[0] * self.tiles[0, rows, :].astype(F32)
        for rank in range(1, 4):
            total = total + weights[rank] * self.tiles[rank, rows, :].astype(F32)
        return total


def side(step):
    return 0 if step == 1 else 1


def last(step):
    return 7 if step == 1 else 0


class Halo:
    def __init__(self, spot, refs):
        self.spot = spot
        (self.tile, self.y_face, self.xy_edge, self.in_z, self.in_x, self.in_y, self.in_zx, self.in_zy, self.in_xy,
         self.in_zxy, self.sems) = refs

    @staticmethod
    def scratch():
        shapes = [(8, 8), (2, 8), (2, 2), (2, 8), (2, 8), (2, 8), (2, 2), (2, 2), (2, 2), (2, 2, 2)]
        return [pltpu.VMEM((*shape, 8, 128), BF16) for shape in shapes] + [pltpu.SemaphoreType.DMA((2, 26))]

    def ends(self, step):
        z, x, y = step
        if y == 0:
            if x == 0:
                return self.tile.at[last(z)], self.in_z.at[side(z)]
            if z == 0:
                return self.tile.at[:, last(x)], self.in_x.at[side(x)]
            return self.tile.at[last(z), last(x)], self.in_zx.at[side(z), side(x)]
        if x == 0:
            if z == 0:
                return self.y_face.at[side(y)], self.in_y.at[side(y)]
            return self.y_face.at[side(y), last(z)], self.in_zy.at[side(z), side(y)]
        if z == 0:
            return self.xy_edge.at[side(x), side(y)], self.in_xy.at[side(x), side(y)]
        return self.xy_edge.at[side(x), side(y)], self.in_zxy.at[side(z), side(x), side(y)]

    def copies(self):
        order = sorted(range(26), key=lambda n: -abs(STEPS[n][2]) * 10 - sum(abs(d) for d in STEPS[n]))
        for n in order:
            source, target = self.ends(STEPS[n])
            yield send(source, target, self.sems.at[0, n], self.sems.at[1, n], self.spot.tile_peer(STEPS[n]))

    def put(self, centre, values):
        rounded = values.astype(BF16).reshape(8, 8, 8, 128)
        self.tile[...] = rounded
        centre[1:9, 1:9] = rounded.astype(F32)
        flat = centre.reshape(800, 128)
        for z in range(8):
            for y in range(2):
                first = ((z + 1) * 10 + 1) * 8 + 7 - 7 * y
                self.y_face[y, z] = flat[pl.ds(first, 8, stride=8), :].astype(BF16)
        for x in range(2):
            for y in range(2):
                first = (10 + 8 - 7 * x) * 8 + 7 - 7 * y
                self.xy_edge[x, y] = flat[pl.ds(first, 8, stride=80), :].astype(BF16)

    def start(self):
        for copy in self.copies():
            copy.start()

    def finish(self, centre, lines, masks, cols):
        for copy in self.copies():
            copy.wait_recv()
        on_z, on_x, on_y = masks
        ends = (0, 9)
        for s in range(2):
            centre[ends[s], 1:9] = self.in_z[s].astype(F32) * on_z[s]
            centre[1:9, ends[s]] = self.in_x[s].astype(F32) * on_x[s]
            lines[s, 1:9, 0:8] = self.in_y[s].astype(F32) * on_y[s]
            for r in range(2):
                centre[ends[s], ends[r]] = self.in_zx[s, r].astype(F32) * (on_z[s] * on_x[r])
                lines[r, ends[s], 0:8] = self.in_zy[s, r].astype(F32) * (on_z[s] * on_y[r])
                rows = self.in_xy[s, r].astype(F32) * (on_x[s] * on_y[r])
                for z in range(8):
                    lines[r, 1 + z, 8 + s : 9 + s] = rows[z : z + 1]
                for q in range(2):
                    rows = self.in_zxy[s, r, q].astype(F32) * (on_z[s] * on_x[r] * on_y[q])
                    row = 7 - 7 * s
                    lines[q, ends[s], 8 + r : 9 + r] = rows[row : row + 1]
        row_id = lax.broadcasted_iota(jnp.int32, (8, 128), 0)

        @pl.loop(0, 10)
        def _(z):
            runs = ([], [], [])
            for x in range(10):
                place = 8 if x == 0 else 9 if x == 9 else x - 1
                middle = centre[z, x]
                low = jnp.broadcast_to(lines[0, z, place : place + 1], (8, 128))
                high = jnp.broadcast_to(lines[1, z, place : place + 1], (8, 128))
                runs[0].append(jnp.where(row_id == 0, low, pltpu.roll(middle, 1, 0)))
                runs[1].append(middle)
                runs[2].append(jnp.where(row_id == 7, high, pltpu.roll(middle, 7, 0)))
            for x in range(3):
                for y in range(3):
                    block = jnp.concatenate(runs[y][x : x + 8], axis=0).astype(BF16)
                    cols[z, :, (3 * x + y) * 128 : (3 * x + y + 1) * 128] = block

    def drain(self):
        for copy in self.copies():
            copy.wait_send()


class Scatter:
    def __init__(self, spot, refs):
        self.spot = spot
        (self.halves, self.partner, self.merged, self.plane_in, self.deep_out, self.deep_in, self.sems,
         self.plane_sems, self.deep_sems) = refs

    @staticmethod
    def scratch():
        return [
            pltpu.VMEM((2, PLANE, DEEP, PIECE, 128), BF16),
            pltpu.VMEM((PLANE, DEEP, PIECE, 128), BF16),
            pltpu.VMEM((PLANE, DEEP, PIECE, 128), BF16),
            pltpu.VMEM((PLANE, DEEP, PIECE, 128), BF16),
            pltpu.VMEM((DEEP, PIECE, 128), BF16),
            pltpu.VMEM((DEEP, PIECE, 128), BF16),
            pltpu.SemaphoreType.DMA((2,)),
            pltpu.SemaphoreType.DMA((2, 16)),
            pltpu.SemaphoreType.DMA((2, 16)),
        ]

    def cut(self, grad_ref):

        @pl.loop(0, DEEP)
        def _(z):
            rows = grad_ref[pl.ds(pl.multiple_of(z * 216, 8), 216), :]
            rows = jnp.concatenate([rows, jnp.zeros((8, 128), F32)], axis=0)
            for column in range(8):
                for part in range(4):
                    first = column * 27 + part * 27 // 4
                    self.halves[part % 2, column * 2 + part // 2, z] = rows[first : first + 8].astype(BF16)

    def pair_copy(self):
        spot = self.spot
        other = 1 - spot.core
        return send(self.halves.at[other], self.partner, self.sems.at[0], self.sems.at[1],
                    spot.column_peer(spot.x_lo * 2 + other))

    def merge(self):
        self.pair_copy().wait_recv()
        core = self.spot.core

        @pl.loop(0, PLANE)
        def _(rank):
            both = self.halves[core, rank].astype(F32) + self.partner[rank].astype(F32)
            self.merged[rank] = both.astype(BF16)

        @pl.loop(1, PLANE)
        def _(step):
            self.plane_copy(step).start()

    def plane_copy(self, step):
        me = self.spot.plane
        rank = (me + step) % PLANE
        return send(self.merged.at[rank], self.plane_in.at[me], self.plane_sems.at[0, rank], self.plane_sems.at[1, me],
                    self.spot.plane_peer(rank))

    def plane_arrival(self, step):
        me = self.spot.plane
        rank = (me + step) % PLANE
        return send(self.merged.at[rank], self.plane_in.at[rank], self.plane_sems.at[0, rank],
                    self.plane_sems.at[1, rank], self.spot.plane_peer(rank))

    def plane_finish(self):
        me = self.spot.plane
        self.plane_in[me] = self.merged[me]

        @pl.loop(1, PLANE)
        def _(step):
            self.plane_arrival(step).wait_recv()

        @pl.loop(0, DEEP)
        def _(z):
            total = jnp.zeros((PIECE, 128), F32)
            for rank in range(PLANE):
                total = total + self.plane_in[rank, z].astype(F32)
            self.deep_out[z] = total.astype(BF16)

        @pl.loop(0, DEEP - 1)
        def _(step):
            self.deep_copy(step).start()

    def deep_copy(self, step):
        me = self.spot.deep
        rank = (me + far_first(step, DEEP)) % DEEP
        return send(self.deep_out.at[rank], self.deep_in.at[me], self.deep_sems.at[0, rank], self.deep_sems.at[1, me],
                    self.spot.deep_peer(rank))

    def deep_arrival(self, step):
        me = self.spot.deep
        rank = (me + far_first(step, DEEP)) % DEEP
        return send(self.deep_out.at[rank], self.deep_in.at[rank], self.deep_sems.at[0, rank],
                    self.deep_sems.at[1, rank], self.spot.deep_peer(rank))

    def deep_finish(self, out_ref):
        me = self.spot.deep
        self.deep_in[me] = self.deep_out[me]

        @pl.loop(0, DEEP - 1)
        def _(step):
            self.deep_arrival(step).wait_recv()

        total = jnp.zeros((PIECE, 128), F32)
        for rank in range(DEEP):
            total = total + self.deep_in[rank].astype(F32)
        total = total * (1.0 / 512)
        lane = lax.broadcasted_iota(jnp.int32, (PIECE, 128), 1)
        share = total
        for depth in range(1, 4):
            ahead = 128 - 32 * depth
            turned = pltpu.roll(total, 128 - ahead, 1)
            moved = jnp.where(lane < 128 - ahead, turned, pltpu.roll(turned, 7, 0))
            share = jnp.where(self.spot.depth == depth, moved, share)
        out_ref[...] = share

    def drain(self):
        self.pair_copy().wait_send()

        @pl.loop(1, PLANE)
        def _(step):
            self.plane_copy(step).wait_send()

        @pl.loop(0, DEEP - 1)
        def _(step):
            self.deep_copy(step).wait_send()


def convolve(cols, kernel_ref):
    total = None
    for z in range(3):
        rows = cols[z : z + 8].reshape(512, 9 * 128)
        term = jnp.dot(rows, kernel_ref[z], preferred_element_type=F32)
        total = term if total is None else total + term
    return total


def turn(kernel_ref, turned):
    @pl.loop(0, 27)
    def _(k):
        turned[26 - k] = kernel_ref[k].T


def kernel_gradient(cols, delta, grad_ref):
    for z in range(3):
        rows = cols[z : z + 8].reshape(512, 9 * 128)
        grad_ref[z * 1152 : (z + 1) * 1152] = lax.dot_general(
            rows, delta, (((0,), (0,)), ((), ())), preferred_element_type=F32
        )


def body(features, cotangent, first_hbm, second_hbm, slot_tile, slot_used, grad_out, first_out, second_out, *scratch):
    spot = Spot()
    scratch = list(scratch)

    def take(kind):
        count = len(kind.scratch())
        refs = scratch[:count]
        del scratch[:count]
        return kind(spot, refs)

    source_in, upstream_in, back_in = (take(Gather) for _ in range(3))
    halo_one, halo_two, halo_three, halo_four = (take(Halo) for _ in range(4))
    scatter_one, scatter_two = (take(Scatter) for _ in range(2))
    news = take(News)
    (first_kernel, second_kernel, first_turned, second_turned, centre, lines, source_cols, act_cols, delta_cols, grad_one,
     grad_two, upstream, slope_one, load_sems) = scratch

    me = spot.depth
    loads = [
        pltpu.make_async_copy(features, source_in.tiles.at[me], load_sems.at[0]),
        pltpu.make_async_copy(cotangent, upstream_in.tiles.at[me], load_sems.at[1]),
        pltpu.make_async_copy(second_hbm, second_kernel, load_sems.at[2]),
        pltpu.make_async_copy(first_hbm, first_kernel, load_sems.at[3]),
    ]
    for load in loads:
        load.start()
    greet(spot)
    loads[0].wait()
    source_in.start()
    news.tell(0)

    weights = [jnp.where(slot_tile[0, j] == me, 1.0, 0.0) * slot_used[0, j].astype(F32) for j in range(4)]
    alive = weights[0] + weights[1] + weights[2] + weights[3]
    own_tile = slot_tile[0, me]
    own_used = slot_used[0, me].astype(F32)

    def mask(condition):
        return jnp.where(condition, 1.0, 0.0)

    masks = (
        (mask(spot.depth > 0), mask(spot.depth < 3)),
        (mask(spot.deep > 0), mask(spot.deep < 15)),
        (mask(spot.column > 0), mask(spot.column < 7)),
    )
    for load in loads[1:]:
        load.wait()
    turn(second_kernel, second_turned)
    first_taps = first_kernel.reshape(3, 1152, 128)
    second_taps = second_kernel.reshape(3, 1152, 128)
    first_back = first_turned.reshape(3, 1152, 128)
    second_back = second_turned.reshape(3, 1152, 128)

    source_in.relay()
    source_in.finish()
    halo_one.put(centre, source_in.pick(weights, slice(None)))
    halo_one.start()
    upstream_in.start()
    turn(first_kernel, first_turned)
    news.hear(0)
    news.tell(1)
    halo_one.finish(centre, lines, masks, source_cols)
    act, slope = gelu_terms(convolve(source_cols, first_taps))
    slope_one[...] = slope * alive
    halo_two.put(centre, act * alive)
    halo_two.start()
    upstream_in.relay()
    news.hear(1)
    news.tell(2)
    upstream_in.finish()
    upstream[...] = upstream_in.pick(weights, slice(None))
    halo_two.finish(centre, lines, masks, act_cols)
    _, slope = gelu_terms(convolve(act_cols, second_taps))
    halo_three.put(centre, upstream[...] * slope * alive)
    halo_three.start()
    kernel_gradient(act_cols, halo_three.tile[...].reshape(512, 128), grad_two)
    scatter_two.cut(grad_two)
    scatter_two.pair_copy().start()
    news.hear(2)
    scatter_two.merge()
    halo_three.finish(centre, lines, masks, delta_cols)
    halo_four.put(centre, convolve(delta_cols, second_back) * slope_one[...])
    halo_four.start()
    kernel_gradient(source_cols, halo_four.tile[...].reshape(512, 128), grad_one)
    scatter_one.cut(grad_one)
    scatter_one.pair_copy().start()
    scatter_one.merge()
    halo_four.finish(centre, lines, masks, delta_cols)
    back_in.tiles[me] = convolve(delta_cols, first_back).astype(BF16)
    back_in.start()
    scatter_two.plane_finish()
    scatter_one.plane_finish()
    scatter_two.deep_finish(second_out)
    back_in.relay()
    back_in.finish()
    picks = [mask(own_tile == t) * own_used for t in range(4)]
    grad_out[...] = back_in.pick(picks, slice(None)).astype(BF16)
    scatter_one.deep_finish(first_out)
    for gather in (source_in, upstream_in, back_in):
        gather.drain()
    for halo in (halo_one, halo_two, halo_three, halo_four):
        halo.drain()
    scatter_two.drain()
    scatter_one.drain()


def hand_out(grad, first, second, grad_out, first_out, second_out):
    grad_out[...] = grad[...]
    for source, target in ((first, first_out), (second, second_out)):
        for row in range(6):
            target[row * 128 : (row + 1) * 128] = source[row]
        target[768:864] = source[6, :96]


def fused(features, cotangent, first_kernel, second_kernel, slot_tile, slot_used):
    whole = pl.BlockSpec(memory_space=pltpu.VMEM)
    left = pl.BlockSpec(memory_space=pl.ANY)
    small = pl.BlockSpec(memory_space=pltpu.SMEM)
    piece = jax.ShapeDtypeStruct((PIECE, 128), F32)
    cols = pltpu.VMEM((10, 64, 9 * 128), BF16)
    kernel = pltpu.VMEM((27, 128, 128), BF16)
    scratch = Gather.scratch() * 3 + Halo.scratch() * 4 + Scatter.scratch() * 2 + News.scratch()
    scratch += [kernel] * 4 + [pltpu.VMEM((10, 10, 8, 128), F32), pltpu.VMEM((2, 10, 16, 128), F32)] + [cols] * 3
    scratch += [pltpu.VMEM((ROWS, 128), F32)] * 2 + [pltpu.VMEM((512, 128), F32)] * 2
    scratch += [pltpu.SemaphoreType.DMA((4,))]
    return pl.pallas_call(
        body,
        out_shape=(jax.ShapeDtypeStruct((512, 128), BF16), piece, piece),
        in_specs=[left, left, left, left, small, small],
        out_specs=(whole, whole, whole),
        scratch_shapes=scratch,
        compiler_params=pltpu.CompilerParams(collective_id=0, has_side_effects=True, vmem_limit_bytes=56 << 20),
    )(features, cotangent, first_kernel, second_kernel, slot_tile, slot_used)


def on_device(features, cotangent, first_kernel, second_kernel, slot_tile, slot_used):
    sums = fused(
        features.reshape(512, 128), cotangent.reshape(512, 128), first_kernel, second_kernel, slot_tile, slot_used
    )
    share = jax.ShapeDtypeStruct((ROWS // 4,), F32)
    whole = pl.BlockSpec(memory_space=pltpu.VMEM)
    grad, first, second = pl.pallas_call(
        hand_out,
        out_shape=(jax.ShapeDtypeStruct((512, 128), BF16), share, share),
        in_specs=[whole] * 3,
        out_specs=(whole,) * 3,
    )(*sums)
    return (grad.reshape(features.shape), first, second)


def solution(mesh):
    tiles = P("space", "depth", None, None)
    slots = P("space", None)
    share = P(("space", "depth"))
    return jax.shard_map(
        on_device,
        mesh=mesh,
        in_specs=(tiles, tiles, P(), P(), slots, slots),
        out_specs=(tiles, share, share),
        check_vma=False,
    )
```

```python
import itertools

import jax
import jax.numpy as jnp
from jax import lax
from jax.experimental import pallas as pl
from jax.experimental.pallas import tpu as pltpu
from jax.sharding import PartitionSpec as P

MESH = pl.DeviceIdType.MESH
SLOPE_COEF = 0.7978845608028654
CUBIC_COEF = 0.044715
PLANE = 16
DEEP = 16
PIECE = 8
ROWS = 27 * 128
STEPS = [d for d in itertools.product((-1, 0, 1), repeat=3) if d != (0, 0, 0)]
PLANE_STEPS = sorted(
    [(x, y) for x in range(4) for y in range(4) if (x, y) != (0, 0)],
    key=lambda step: -min(step[0], 4 - step[0]) - min(step[1], 4 - step[1]),
)
DEEP_STEPS = sorted(range(1, DEEP), key=lambda step: -min(step, DEEP - step))
PARTS = ((0, 5), (5, 10), (10, DEEP))
F32 = jnp.float32
BF16 = jnp.bfloat16


def gelu_terms(values):
    inner = SLOPE_COEF * (values + CUBIC_COEF * values * values * values)
    tangent = jnp.tanh(inner)
    slope = 0.5 * (1.0 + tangent) + 0.5 * values * (1.0 - tangent * tangent) * SLOPE_COEF * (
        1.0 + 3.0 * CUBIC_COEF * values * values
    )
    return 0.5 * values * (1.0 + tangent), slope


class Spot:
    def __init__(self):
        self.space = lax.axis_index("space")
        self.depth = lax.axis_index("depth")
        self.deep = self.space // 8
        self.column = self.space % 8
        self.core = self.depth % 2
        self.x_lo = self.depth // 2
        self.plane = self.column * 2 + self.x_lo

    def plane_step(self, x, y):
        far_x = lax.rem(self.column // 4 * 2 + self.x_lo + x, 4)
        far_y = lax.rem(self.column % 4 + y, 4)
        high, low = lax.div(far_x, 2), lax.rem(far_x, 2)
        column = high * 4 + far_y
        return column * 2 + low, (self.deep * 8 + column, low * 2 + self.core)

    def deep_peer(self, rank):
        return (rank * 8 + self.column, self.depth)

    def column_peer(self, rank):
        return (self.space, rank)

    def tile_peer(self, step):
        z, x, y = step
        return (lax.rem(self.deep + x + 16, 16) * 8 + lax.rem(self.column + y + 8, 8), lax.rem(self.depth + z + 4, 4))


def greet(spot):
    barrier = pltpu.get_barrier_semaphore()

    def tell(peer):
        pl.semaphore_signal(barrier, inc=1, device_id=peer, device_id_type=MESH)

    for step in STEPS:
        tell(spot.tile_peer(step))
    for step in range(1, 4):
        tell(spot.column_peer((spot.depth + step) % 4))
    pl.semaphore_wait(barrier, len(STEPS) + 3)


class News:
    def __init__(self, spot, refs):
        self.spot = spot
        (self.sem,) = refs

    @staticmethod
    def scratch():
        return [pltpu.SemaphoreType.REGULAR((3,))]

    def peers(self, level):
        reach = 2**level
        steps = [(0, reach, 0), (0, -reach, 0), (0, 0, reach)] + ([(0, 0, -reach)] if level < 2 else [])
        return [self.spot.tile_peer(step) for step in steps]

    def tell(self, level):
        for peer in self.peers(level):
            pl.semaphore_signal(self.sem.at[level], inc=1, device_id=peer, device_id_type=MESH)

    def hear(self, level):
        pl.semaphore_wait(self.sem.at[level], len(self.peers(level)))


def send(source, target, send_sem, recv_sem, peer):
    return pltpu.make_async_remote_copy(
        src_ref=source, dst_ref=target, send_sem=send_sem, recv_sem=recv_sem, device_id=peer, device_id_type=MESH
    )


class Gather:
    def __init__(self, spot, refs):
        self.spot = spot
        self.tiles, self.sems = refs
        self.me = spot.depth
        self.pair = spot.x_lo * 2 + 1 - spot.core
        self.across = (1 - spot.x_lo) * 2 + spot.core
        self.diagonal = (1 - spot.x_lo) * 2 + 1 - spot.core

    @staticmethod
    def scratch():
        return [pltpu.VMEM((4, 512, 128), BF16), pltpu.SemaphoreType.DMA((2, 4))]

    def part(self, tile, half, way, peer):
        rows = self.tiles.at[tile] if half is None else self.tiles.at[tile, half * 256 : (half + 1) * 256]
        return send(rows, rows, self.sems.at[0, way], self.sems.at[1, way], self.spot.column_peer(peer))

    def start(self):
        for half in range(2):
            self.part(self.me, half, half, self.across).start()
        self.part(self.me, None, 2, self.pair).start()

    def relay(self):
        for half in range(2):
            self.part(self.across, half, half, self.across).wait_recv()
            self.part(self.across, half, 3, self.pair).start()

    def finish(self):
        self.part(self.pair, None, 2, self.pair).wait_recv()
        self.part(self.diagonal, None, 3, self.pair).wait_recv()

    def drain(self):
        for half in range(2):
            self.part(self.me, half, half, self.across).wait_send()
        self.part(self.me, None, 2, self.pair).wait_send()
        self.part(self.across, None, 3, self.pair).wait_send()

    def pick(self, weights, rows):
        total = weights[0] * self.tiles[0, rows, :].astype(F32)
        for rank in range(1, 4):
            total = total + weights[rank] * self.tiles[rank, rows, :].astype(F32)
        return total


def side(step):
    return 0 if step == 1 else 1


def last(step):
    return 7 if step == 1 else 0


class Halo:
    def __init__(self, spot, refs):
        self.spot = spot
        self.tile, self.y_face, self.xy_edge, self.inbox, self.sems = refs

    @staticmethod
    def scratch():
        shapes = [(8, 8), (2, 8), (2, 2), (68,)]
        return [pltpu.VMEM((*shape, 8, 128), BF16) for shape in shapes] + [pltpu.SemaphoreType.DMA((2,))]

    def face(self, axis, s):
        return self.inbox.at[axis * 16 + s * 8 : axis * 16 + s * 8 + 8]

    def edge(self, plane, s, r):
        return self.inbox.at[48 + plane * 4 + 2 * s + r]

    def corner(self, s, r, q):
        return self.inbox.at[60 + 4 * s + 2 * r + q]

    def ends(self, step):
        z, x, y = step
        if y == 0:
            if x == 0:
                return self.tile.at[last(z)], self.face(0, side(z))
            if z == 0:
                return self.tile.at[:, last(x)], self.face(1, side(x))
            return self.tile.at[last(z), last(x)], self.edge(0, side(z), side(x))
        if x == 0:
            if z == 0:
                return self.y_face.at[side(y)], self.face(2, side(y))
            return self.y_face.at[side(y), last(z)], self.edge(1, side(z), side(y))
        if z == 0:
            return self.xy_edge.at[side(x), side(y)], self.edge(2, side(x), side(y))
        return self.xy_edge.at[side(x), side(y)], self.corner(side(z), side(x), side(y))

    def whole(self):
        return send(self.inbox, self.inbox, self.sems.at[0], self.sems.at[1], self.spot.tile_peer((0, 0, 1)))

    def put(self, centre, values):
        rounded = values.astype(BF16).reshape(8, 8, 8, 128)
        self.tile[...] = rounded
        centre[1:9, 1:9] = rounded.astype(F32)
        flat = centre.reshape(800, 128)
        for z in range(8):
            for y in range(2):
                first = ((z + 1) * 10 + 1) * 8 + 7 - 7 * y
                self.y_face[y, z] = flat[pl.ds(first, 8, stride=8), :].astype(BF16)
        for x in range(2):
            for y in range(2):
                first = (10 + 8 - 7 * x) * 8 + 7 - 7 * y
                self.xy_edge[x, y] = flat[pl.ds(first, 8, stride=80), :].astype(BF16)

    def start(self):
        order = sorted(STEPS, key=lambda step: -abs(step[2]) * 10 - sum(abs(d) for d in step))
        for step in order:
            source, target = self.ends(step)
            send(source, target, self.sems.at[0], self.sems.at[1], self.spot.tile_peer(step)).start()

    def finish(self, centre, lines, masks, cols):
        self.whole().wait_recv()
        on_z, on_x, on_y = masks
        ends = (0, 9)
        for s in range(2):
            centre[ends[s], 1:9] = self.face(0, s)[...].astype(F32) * on_z[s]
            centre[1:9, ends[s]] = self.face(1, s)[...].astype(F32) * on_x[s]
            lines[s, 1:9, 0:8] = self.face(2, s)[...].astype(F32) * on_y[s]
            for r in range(2):
                centre[ends[s], ends[r]] = self.edge(0, s, r)[...].astype(F32) * (on_z[s] * on_x[r])
                lines[r, ends[s], 0:8] = self.edge(1, s, r)[...].astype(F32) * (on_z[s] * on_y[r])
                rows = self.edge(2, s, r)[...].astype(F32) * (on_x[s] * on_y[r])
                for z in range(8):
                    lines[r, 1 + z, 8 + s : 9 + s] = rows[z : z + 1]
                for q in range(2):
                    rows = self.corner(s, r, q)[...].astype(F32) * (on_z[s] * on_x[r] * on_y[q])
                    row = 7 - 7 * s
                    lines[q, ends[s], 8 + r : 9 + r] = rows[row : row + 1]
        row_id = lax.broadcasted_iota(jnp.int32, (8, 128), 0)

        @pl.loop(0, 10)
        def _(z):
            runs = ([], [], [])
            for x in range(10):
                place = 8 if x == 0 else 9 if x == 9 else x - 1
                middle = centre[z, x]
                low = jnp.broadcast_to(lines[0, z, place : place + 1], (8, 128))
                high = jnp.broadcast_to(lines[1, z, place : place + 1], (8, 128))
                runs[0].append(jnp.where(row_id == 0, low, pltpu.roll(middle, 1, 0)))
                runs[1].append(middle)
                runs[2].append(jnp.where(row_id == 7, high, pltpu.roll(middle, 7, 0)))
            for x in range(3):
                for y in range(3):
                    block = jnp.concatenate(runs[y][x : x + 8], axis=0).astype(BF16)
                    cols[z, :, (3 * x + y) * 128 : (3 * x + y + 1) * 128] = block

    def drain(self):
        self.whole().wait_send()


class Scatter:
    def __init__(self, spot, refs):
        self.spot = spot
        (self.halves, self.partner, self.merged, self.plane_in, self.deep_out, self.deep_in, self.grad, self.pair_sems,
         self.plane_sems, self.deep_sems) = refs

    @staticmethod
    def scratch():
        return [
            pltpu.VMEM((2, PLANE, DEEP, PIECE, 128), BF16),
            pltpu.VMEM((PLANE, DEEP, PIECE, 128), BF16),
            pltpu.VMEM((PLANE, DEEP, PIECE, 128), BF16),
            pltpu.VMEM((PLANE, DEEP, PIECE, 128), BF16),
            pltpu.VMEM((DEEP, PIECE, 128), BF16),
            pltpu.VMEM((DEEP, PIECE, 128), BF16),
            pltpu.VMEM((ROWS, 128), F32),
            pltpu.SemaphoreType.DMA((2, len(PARTS))),
            pltpu.SemaphoreType.DMA((2,)),
            pltpu.SemaphoreType.DMA((2,)),
        ]

    def produce(self, cols, delta):
        for part, (first, end) in enumerate(PARTS):
            rows = cols[part : part + 8].reshape(512, 9 * 128)
            self.grad[part * 1152 : (part + 1) * 1152] = lax.dot_general(
                rows, delta, (((0,), (0,)), ((), ())), preferred_element_type=F32
            )
            self.cut(first, end)
            self.pair_copy(part).start()

    def cut(self, first_z, end_z):

        @pl.loop(first_z, end_z)
        def _(z):
            rows = self.grad[pl.ds(pl.multiple_of(z * 216, 8), 216), :]
            rows = jnp.concatenate([rows, jnp.zeros((8, 128), F32)], axis=0)
            for column in range(8):
                for part in range(4):
                    first = column * 27 + part * 27 // 4
                    self.halves[part % 2, column * 2 + part // 2, z] = rows[first : first + 8].astype(BF16)

    def pair_copy(self, part):
        spot = self.spot
        other = 1 - spot.core
        first, end = PARTS[part]
        return send(self.halves.at[other, :, first:end], self.partner.at[:, first:end], self.pair_sems.at[0, part],
                    self.pair_sems.at[1, part], spot.column_peer(spot.x_lo * 2 + other))

    def merge(self, together):
        core = self.spot.core
        for part, (first, end) in enumerate(PARTS):
            self.pair_copy(part).wait_recv()
            for rank in range(PLANE):
                own = self.halves[core, rank, first:end].astype(F32)
                both = own + self.partner[rank, first:end].astype(F32)
                self.merged[rank, first:end] = both.astype(BF16)
            if not together:
                self.plane_start(first, end)
        if together:
            self.plane_start(0, DEEP)

    def plane_start(self, first, end):
        spot = self.spot
        for x, y in PLANE_STEPS:
            rank, peer = spot.plane_step(x, y)
            send(self.merged.at[rank, first:end], self.plane_in.at[spot.plane, first:end], self.plane_sems.at[0],
                 self.plane_sems.at[1], peer).start()

    def plane_whole(self):
        return send(self.merged.at[0 : PLANE - 1], self.plane_in.at[0 : PLANE - 1], self.plane_sems.at[0],
                    self.plane_sems.at[1], self.spot.plane_step(1, 0)[1])

    def plane_finish(self):
        me = self.spot.plane
        self.plane_in[me] = self.merged[me]
        self.plane_whole().wait_recv()

        @pl.loop(0, DEEP)
        def _(z):
            total = jnp.zeros((PIECE, 128), F32)
            for rank in range(PLANE):
                total = total + self.plane_in[rank, z].astype(F32)
            self.deep_out[z] = total.astype(BF16)

        for step in DEEP_STEPS:
            rank = lax.rem(self.spot.deep + step, DEEP)
            send(self.deep_out.at[rank], self.deep_in.at[self.spot.deep], self.deep_sems.at[0], self.deep_sems.at[1],
                 self.spot.deep_peer(rank)).start()

    def deep_whole(self):
        return send(self.deep_out.at[0 : DEEP - 1], self.deep_in.at[0 : DEEP - 1], self.deep_sems.at[0],
                    self.deep_sems.at[1], self.spot.deep_peer(lax.rem(self.spot.deep + 1, DEEP)))

    def deep_finish(self, out_ref):
        me = self.spot.deep
        self.deep_in[me] = self.deep_out[me]
        self.deep_whole().wait_recv()

        total = jnp.zeros((PIECE, 128), F32)
        for rank in range(DEEP):
            total = total + self.deep_in[rank].astype(F32)
        total = total * (1.0 / 512)
        lane = lax.broadcasted_iota(jnp.int32, (PIECE, 128), 1)
        share = total
        for depth in range(1, 4):
            ahead = 128 - 32 * depth
            turned = pltpu.roll(total, 128 - ahead, 1)
            moved = jnp.where(lane < 128 - ahead, turned, pltpu.roll(turned, 7, 0))
            share = jnp.where(self.spot.depth == depth, moved, share)
        out_ref[...] = share

    def drain(self):
        for part in range(len(PARTS)):
            self.pair_copy(part).wait_send()
        self.plane_whole().wait_send()
        self.deep_whole().wait_send()


def convolve(cols, kernel_ref):
    total = None
    for z in range(3):
        rows = cols[z : z + 8].reshape(512, 9 * 128)
        term = jnp.dot(rows, kernel_ref[z], preferred_element_type=F32)
        total = term if total is None else total + term
    return total


def turn(kernel_ref, turned):
    @pl.loop(0, 27)
    def _(k):
        turned[26 - k] = kernel_ref[k].T


def body(features, cotangent, first_hbm, second_hbm, tile_hbm, used_hbm, grad_out, first_out, second_out, *scratch):
    spot = Spot()
    scratch = list(scratch)

    def take(kind):
        count = len(kind.scratch())
        refs = scratch[:count]
        del scratch[:count]
        return kind(spot, refs)

    source_in, upstream_in, back_in = (take(Gather) for _ in range(3))
    halo_one, halo_two, halo_three, halo_four = (take(Halo) for _ in range(4))
    scatter_one, scatter_two = (take(Scatter) for _ in range(2))
    news = take(News)
    (first_kernel, second_kernel, first_turned, second_turned, centre, lines, source_cols, act_cols, delta_cols, upstream,
     slope_one, slot_tile, slot_used, load_sems) = scratch

    me = spot.depth
    loads = [
        pltpu.make_async_copy(features, source_in.tiles.at[me], load_sems.at[0]),
        pltpu.make_async_copy(tile_hbm, slot_tile, load_sems.at[4]),
        pltpu.make_async_copy(used_hbm, slot_used, load_sems.at[5]),
        pltpu.make_async_copy(cotangent, upstream_in.tiles.at[me], load_sems.at[1]),
        pltpu.make_async_copy(second_hbm, second_kernel, load_sems.at[2]),
        pltpu.make_async_copy(first_hbm, first_kernel, load_sems.at[3]),
    ]
    for load in loads:
        load.start()
    greet(spot)
    loads[0].wait()
    source_in.start()
    news.tell(0)
    for load in loads[1:3]:
        load.wait()

    weights = [jnp.where(slot_tile[0, j] == me, 1.0, 0.0) * slot_used[0, j].astype(F32) for j in range(4)]
    alive = weights[0] + weights[1] + weights[2] + weights[3]
    own_tile = slot_tile[0, me]
    own_used = slot_used[0, me].astype(F32)

    def mask(condition):
        return jnp.where(condition, 1.0, 0.0)

    masks = (
        (mask(spot.depth > 0), mask(spot.depth < 3)),
        (mask(spot.deep > 0), mask(spot.deep < 15)),
        (mask(spot.column > 0), mask(spot.column < 7)),
    )
    first_taps = first_kernel.reshape(3, 1152, 128)
    second_taps = second_kernel.reshape(3, 1152, 128)
    first_back = first_turned.reshape(3, 1152, 128)
    second_back = second_turned.reshape(3, 1152, 128)

    source_in.relay()
    source_in.finish()
    halo_one.put(centre, source_in.pick(weights, slice(None)))
    halo_one.start()
    for load in loads[3:]:
        load.wait()
    upstream_in.start()
    turn(first_kernel, first_turned)
    news.hear(0)
    news.tell(1)
    halo_one.finish(centre, lines, masks, source_cols)
    act, slope = gelu_terms(convolve(source_cols, first_taps))
    slope_one[...] = slope * alive
    halo_two.put(centre, act * alive)
    halo_two.start()
    upstream_in.relay()
    news.hear(1)
    news.tell(2)
    turn(second_kernel, second_turned)
    upstream_in.finish()
    upstream[...] = upstream_in.pick(weights, slice(None))
    halo_two.finish(centre, lines, masks, act_cols)
    _, slope = gelu_terms(convolve(act_cols, second_taps))
    halo_three.put(centre, upstream[...] * slope * alive)
    halo_three.start()
    scatter_two.produce(act_cols, halo_three.tile[...].reshape(512, 128))
    news.hear(2)
    halo_three.finish(centre, lines, masks, delta_cols)
    scatter_two.merge(together=True)
    halo_four.put(centre, convolve(delta_cols, second_back) * slope_one[...])
    halo_four.start()
    scatter_one.produce(source_cols, halo_four.tile[...].reshape(512, 128))
    scatter_one.merge(together=False)
    halo_four.finish(centre, lines, masks, delta_cols)
    back_in.tiles[me] = convolve(delta_cols, first_back).astype(BF16)
    back_in.start()
    scatter_two.plane_finish()
    scatter_one.plane_finish()
    scatter_two.deep_finish(second_out)
    back_in.relay()
    back_in.finish()
    picks = [mask(own_tile == t) * own_used for t in range(4)]
    grad_out[...] = back_in.pick(picks, slice(None)).astype(BF16)
    scatter_one.deep_finish(first_out)
    for gather in (source_in, upstream_in, back_in):
        gather.drain()
    for halo in (halo_one, halo_two, halo_three, halo_four):
        halo.drain()
    scatter_two.drain()
    scatter_one.drain()


def hand_out(grad, first, second, grad_out, first_out, second_out):
    grad_out[...] = grad[...]
    for source, target in ((first, first_out), (second, second_out)):
        for row in range(6):
            target[row * 128 : (row + 1) * 128] = source[row]
        target[768:864] = source[6, :96]


def fused(features, cotangent, first_kernel, second_kernel, slot_tile, slot_used):
    whole = pl.BlockSpec(memory_space=pltpu.VMEM)
    left = pl.BlockSpec(memory_space=pl.ANY)
    piece = pltpu.VMEM((PIECE, 128), F32)
    cols = pltpu.VMEM((10, 64, 9 * 128), BF16)
    kernel = pltpu.VMEM((27, 128, 128), BF16)
    scratch = Gather.scratch() * 3 + Halo.scratch() * 4 + Scatter.scratch() * 2 + News.scratch()
    scratch += [kernel] * 4 + [pltpu.VMEM((10, 10, 8, 128), F32), pltpu.VMEM((2, 10, 16, 128), F32)] + [cols] * 3
    scratch += [pltpu.VMEM((512, 128), F32)] * 2 + [pltpu.SMEM((1, 4), jnp.int32)] * 2
    scratch += [pltpu.SemaphoreType.DMA((6,))]
    return pl.pallas_call(
        body,
        out_shape=(pltpu.VMEM((512, 128), BF16), piece, piece),
        in_specs=[left] * 6,
        out_specs=(whole, whole, whole),
        scratch_shapes=scratch,
        compiler_params=pltpu.CompilerParams(collective_id=0, has_side_effects=True, vmem_limit_bytes=56 << 20),
    )(features, cotangent, first_kernel, second_kernel, slot_tile, slot_used)


def on_device(features, cotangent, first_kernel, second_kernel, slot_tile, slot_used):
    sums = fused(
        features.reshape(512, 128), cotangent.reshape(512, 128), first_kernel, second_kernel, slot_tile, slot_used
    )
    share = jax.ShapeDtypeStruct((ROWS // 4,), F32)
    whole = pl.BlockSpec(memory_space=pltpu.VMEM)
    grad, first, second = pl.pallas_call(
        hand_out,
        out_shape=(jax.ShapeDtypeStruct((512, 128), BF16), share, share),
        in_specs=[whole] * 3,
        out_specs=(whole,) * 3,
    )(*(pltpu.with_memory_space_constraint(value, pltpu.VMEM) for value in sums))
    return (grad.reshape(features.shape), first, second)


def solution(mesh):
    tiles = P("space", "depth", None, None)
    slots = P("space", None)
    share = P(("space", "depth"))
    return jax.shard_map(
        on_device,
        mesh=mesh,
        in_specs=(tiles, tiles, P(), P(), slots, slots),
        out_specs=(tiles, share, share),
        check_vma=False,
    )
```

```python
import itertools

import jax
import jax.numpy as jnp
from jax import lax
from jax.experimental import pallas as pl
from jax.experimental.pallas import tpu as pltpu
from jax.sharding import PartitionSpec as P

MESH = pl.DeviceIdType.MESH
SLOPE_COEF = 0.7978845608028654
CUBIC_COEF = 0.044715
PLANE = 16
DEEP = 16
PIECE = 8
ROWS = 27 * 128
STEPS = [d for d in itertools.product((-1, 0, 1), repeat=3) if d != (0, 0, 0)]
PLANE_STEPS = sorted(
    [(x, y) for x in range(4) for y in range(4) if (x, y) != (0, 0)],
    key=lambda step: -min(step[0], 4 - step[0]) - min(step[1], 4 - step[1]),
)
DEEP_STEPS = (8, 7, 9, 6, 10, 5, 11, 4, 12, 3, 13, 2, 14, 1, 15)
PARTS = ((0, 5), (5, 10), (10, DEEP))
F32 = jnp.float32
BF16 = jnp.bfloat16


def gelu_terms(values):
    inner = SLOPE_COEF * (values + CUBIC_COEF * values * values * values)
    tangent = jnp.tanh(inner)
    slope = 0.5 * (1.0 + tangent) + 0.5 * values * (1.0 - tangent * tangent) * SLOPE_COEF * (
        1.0 + 3.0 * CUBIC_COEF * values * values
    )
    return 0.5 * values * (1.0 + tangent), slope


class Spot:
    def __init__(self):
        self.space = lax.axis_index("space")
        self.depth = lax.axis_index("depth")
        self.deep = self.space // 8
        self.column = self.space % 8
        self.core = self.depth % 2
        self.x_lo = self.depth // 2
        self.plane = self.column * 2 + self.x_lo

    def plane_step(self, x, y):
        far_x = lax.rem(self.column // 4 * 2 + self.x_lo + x, 4)
        far_y = lax.rem(self.column % 4 + y, 4)
        high, low = lax.div(far_x, 2), lax.rem(far_x, 2)
        column = high * 4 + far_y
        return column * 2 + low, (self.deep * 8 + column, low * 2 + self.core)

    def deep_peer(self, rank):
        return (rank * 8 + self.column, self.depth)

    def column_peer(self, rank):
        return (self.space, rank)

    def tile_peer(self, step):
        z, x, y = step
        return (lax.rem(self.deep + x + 16, 16) * 8 + lax.rem(self.column + y + 8, 8), lax.rem(self.depth + z + 4, 4))


def greet(spot):
    barrier = pltpu.get_barrier_semaphore()

    def tell(peer):
        pl.semaphore_signal(barrier, inc=1, device_id=peer, device_id_type=MESH)

    for step in STEPS:
        tell(spot.tile_peer(step))
    for step in range(1, 4):
        tell(spot.column_peer((spot.depth + step) % 4))
    pl.semaphore_wait(barrier, len(STEPS) + 3)


class News:
    def __init__(self, spot, refs):
        self.spot = spot
        (self.sem,) = refs

    @staticmethod
    def scratch():
        return [pltpu.SemaphoreType.REGULAR((3,))]

    def peers(self, level):
        reach = 2**level
        steps = [(0, reach, 0), (0, -reach, 0), (0, 0, reach)] + ([(0, 0, -reach)] if level < 2 else [])
        return [self.spot.tile_peer(step) for step in steps]

    def tell(self, level):
        for peer in self.peers(level):
            pl.semaphore_signal(self.sem.at[level], inc=1, device_id=peer, device_id_type=MESH)

    def hear(self, level):
        pl.semaphore_wait(self.sem.at[level], len(self.peers(level)))


def send(source, target, send_sem, recv_sem, peer):
    return pltpu.make_async_remote_copy(
        src_ref=source, dst_ref=target, send_sem=send_sem, recv_sem=recv_sem, device_id=peer, device_id_type=MESH
    )


class Gather:
    def __init__(self, spot, refs):
        self.spot = spot
        self.tiles, self.sems = refs
        self.me = spot.depth
        self.pair = spot.x_lo * 2 + 1 - spot.core
        self.across = (1 - spot.x_lo) * 2 + spot.core
        self.diagonal = (1 - spot.x_lo) * 2 + 1 - spot.core

    @staticmethod
    def scratch():
        return [pltpu.VMEM((4, 512, 128), BF16), pltpu.SemaphoreType.DMA((2, 4))]

    def part(self, tile, half, way, peer):
        rows = self.tiles.at[tile] if half is None else self.tiles.at[tile, half * 256 : (half + 1) * 256]
        return send(rows, rows, self.sems.at[0, way], self.sems.at[1, way], self.spot.column_peer(peer))

    def start(self):
        for half in range(2):
            self.part(self.me, half, half, self.across).start()
        self.part(self.me, None, 2, self.pair).start()

    def relay(self):
        for half in range(2):
            self.part(self.across, half, half, self.across).wait_recv()
            self.part(self.across, half, 3, self.pair).start()

    def finish(self):
        self.part(self.pair, None, 2, self.pair).wait_recv()
        self.part(self.diagonal, None, 3, self.pair).wait_recv()

    def drain(self):
        for half in range(2):
            self.part(self.me, half, half, self.across).wait_send()
        self.part(self.me, None, 2, self.pair).wait_send()
        self.part(self.across, None, 3, self.pair).wait_send()

    def pick(self, weights, rows):
        total = weights[0] * self.tiles[0, rows, :].astype(F32)
        for rank in range(1, 4):
            total = total + weights[rank] * self.tiles[rank, rows, :].astype(F32)
        return total


def side(step):
    return 0 if step == 1 else 1


def last(step):
    return 7 if step == 1 else 0


class Halo:
    def __init__(self, spot, refs):
        self.spot = spot
        self.tile, self.y_face, self.xy_edge, self.inbox, self.sems = refs

    @staticmethod
    def scratch():
        shapes = [(8, 8), (2, 8), (2, 2), (68,)]
        return [pltpu.VMEM((*shape, 8, 128), BF16) for shape in shapes] + [pltpu.SemaphoreType.DMA((2,))]

    def face(self, axis, s):
        return self.inbox.at[axis * 16 + s * 8 : axis * 16 + s * 8 + 8]

    def edge(self, plane, s, r):
        return self.inbox.at[48 + plane * 4 + 2 * s + r]

    def corner(self, s, r, q):
        return self.inbox.at[60 + 4 * s + 2 * r + q]

    def ends(self, step):
        z, x, y = step
        if y == 0:
            if x == 0:
                return self.tile.at[last(z)], self.face(0, side(z))
            if z == 0:
                return self.tile.at[:, last(x)], self.face(1, side(x))
            return self.tile.at[last(z), last(x)], self.edge(0, side(z), side(x))
        if x == 0:
            if z == 0:
                return self.y_face.at[side(y)], self.face(2, side(y))
            return self.y_face.at[side(y), last(z)], self.edge(1, side(z), side(y))
        if z == 0:
            return self.xy_edge.at[side(x), side(y)], self.edge(2, side(x), side(y))
        return self.xy_edge.at[side(x), side(y)], self.corner(side(z), side(x), side(y))

    def whole(self):
        return send(self.inbox, self.inbox, self.sems.at[0], self.sems.at[1], self.spot.tile_peer((0, 0, 1)))

    def put(self, centre, values):
        rounded = values.astype(BF16).reshape(8, 8, 8, 128)
        self.tile[...] = rounded
        centre[1:9, 1:9] = rounded.astype(F32)
        flat = centre.reshape(800, 128)
        for z in range(8):
            for y in range(2):
                first = ((z + 1) * 10 + 1) * 8 + 7 - 7 * y
                self.y_face[y, z] = flat[pl.ds(first, 8, stride=8), :].astype(BF16)
        for x in range(2):
            for y in range(2):
                first = (10 + 8 - 7 * x) * 8 + 7 - 7 * y
                self.xy_edge[x, y] = flat[pl.ds(first, 8, stride=80), :].astype(BF16)

    def start(self):
        order = sorted(STEPS, key=lambda step: -abs(step[2]) * 10 - sum(abs(d) for d in step))
        for step in order:
            source, target = self.ends(step)
            send(source, target, self.sems.at[0], self.sems.at[1], self.spot.tile_peer(step)).start()

    def finish(self, centre, lines, masks, cols):
        self.whole().wait_recv()
        on_z, on_x, on_y = masks
        ends = (0, 9)
        for s in range(2):
            centre[ends[s], 1:9] = self.face(0, s)[...].astype(F32) * on_z[s]
            centre[1:9, ends[s]] = self.face(1, s)[...].astype(F32) * on_x[s]
            lines[s, 1:9, 0:8] = self.face(2, s)[...].astype(F32) * on_y[s]
            for r in range(2):
                centre[ends[s], ends[r]] = self.edge(0, s, r)[...].astype(F32) * (on_z[s] * on_x[r])
                lines[r, ends[s], 0:8] = self.edge(1, s, r)[...].astype(F32) * (on_z[s] * on_y[r])
                rows = self.edge(2, s, r)[...].astype(F32) * (on_x[s] * on_y[r])
                for z in range(8):
                    lines[r, 1 + z, 8 + s : 9 + s] = rows[z : z + 1]
                for q in range(2):
                    rows = self.corner(s, r, q)[...].astype(F32) * (on_z[s] * on_x[r] * on_y[q])
                    row = 7 - 7 * s
                    lines[q, ends[s], 8 + r : 9 + r] = rows[row : row + 1]
        row_id = lax.broadcasted_iota(jnp.int32, (8, 128), 0)

        @pl.loop(0, 10)
        def _(z):
            runs = ([], [], [])
            for x in range(10):
                place = 8 if x == 0 else 9 if x == 9 else x - 1
                middle = centre[z, x]
                low = jnp.broadcast_to(lines[0, z, place : place + 1], (8, 128))
                high = jnp.broadcast_to(lines[1, z, place : place + 1], (8, 128))
                runs[0].append(jnp.where(row_id == 0, low, pltpu.roll(middle, 1, 0)))
                runs[1].append(middle)
                runs[2].append(jnp.where(row_id == 7, high, pltpu.roll(middle, 7, 0)))
            for x in range(3):
                for y in range(3):
                    block = jnp.concatenate(runs[y][x : x + 8], axis=0).astype(BF16)
                    cols[z, :, (3 * x + y) * 128 : (3 * x + y + 1) * 128] = block

    def drain(self):
        self.whole().wait_send()


class Scatter:
    def __init__(self, spot, refs):
        self.spot = spot
        (self.halves, self.partner, self.merged, self.plane_in, self.deep_out, self.deep_in, self.grad, self.pair_sems,
         self.plane_sems, self.deep_sems) = refs

    @staticmethod
    def scratch():
        return [
            pltpu.VMEM((2, PLANE, DEEP, PIECE, 128), BF16),
            pltpu.VMEM((PLANE, DEEP, PIECE, 128), BF16),
            pltpu.VMEM((PLANE, DEEP, PIECE, 128), BF16),
            pltpu.VMEM((PLANE, DEEP, PIECE, 128), BF16),
            pltpu.VMEM((DEEP, PIECE, 128), BF16),
            pltpu.VMEM((DEEP, PIECE, 128), BF16),
            pltpu.VMEM((ROWS, 128), F32),
            pltpu.SemaphoreType.DMA((2, len(PARTS))),
            pltpu.SemaphoreType.DMA((2, len(PARTS))),
            pltpu.SemaphoreType.DMA((2,)),
        ]

    def produce(self, cols, delta):
        for part, (first, end) in enumerate(PARTS):
            rows = cols[part : part + 8].reshape(512, 9 * 128)
            self.grad[part * 1152 : (part + 1) * 1152] = lax.dot_general(
                rows, delta, (((0,), (0,)), ((), ())), preferred_element_type=F32
            )
            self.cut(first, end)
            self.pair_copy(part).start()

    def place(self, z):
        return z

    def cut(self, first_z, end_z):

        @pl.loop(first_z, end_z)
        def _(z):
            place = self.place(z)
            rows = self.grad[pl.ds(pl.multiple_of(z * 216, 8), 216), :]
            rows = jnp.concatenate([rows, jnp.zeros((8, 128), F32)], axis=0)
            for column in range(8):
                for part in range(4):
                    first = column * 27 + part * 27 // 4
                    self.halves[part % 2, column * 2 + part // 2, place] = rows[first : first + 8].astype(BF16)

    def pair_copy(self, part):
        spot = self.spot
        other = 1 - spot.core
        first, end = PARTS[part]
        return send(self.halves.at[other, :, first:end], self.partner.at[:, first:end], self.pair_sems.at[0, part],
                    self.pair_sems.at[1, part], spot.column_peer(spot.x_lo * 2 + other))

    def merge_part(self, part):
        core = self.spot.core
        first, end = PARTS[part]
        self.pair_copy(part).wait_recv()
        for rank in range(PLANE):
            own = self.halves[core, rank, first:end].astype(F32)
            both = own + self.partner[rank, first:end].astype(F32)
            self.merged[rank, first:end] = both.astype(BF16)

    def merge(self):
        for part in range(len(PARTS)):
            self.merge_part(part)
        self.plane_start(0, 0, DEEP)

    def plane_start(self, part, first, end):
        spot = self.spot
        for x, y in PLANE_STEPS:
            rank, peer = spot.plane_step(x, y)
            send(self.merged.at[rank, first:end], self.plane_in.at[spot.plane, first:end], self.plane_sems.at[0, part],
                 self.plane_sems.at[1, part], peer).start()

    def plane_whole(self, part, first, end):
        return send(self.merged.at[0 : PLANE - 1, first:end], self.plane_in.at[0 : PLANE - 1, first:end],
                    self.plane_sems.at[0, part], self.plane_sems.at[1, part], self.spot.plane_step(1, 0)[1])

    def plane_finish(self):
        me = self.spot.plane
        self.plane_in[me] = self.merged[me]
        self.plane_whole(0, 0, DEEP).wait_recv()

        @pl.loop(0, DEEP)
        def _(z):
            total = jnp.zeros((PIECE, 128), F32)
            for rank in range(PLANE):
                total = total + self.plane_in[rank, z].astype(F32)
            self.deep_out[z] = total.astype(BF16)

        for step in DEEP_STEPS:
            rank = lax.rem(self.spot.deep + step, DEEP)
            send(self.deep_out.at[rank], self.deep_in.at[self.spot.deep], self.deep_sems.at[0], self.deep_sems.at[1],
                 self.spot.deep_peer(rank)).start()

    def deep_whole(self):
        return send(self.deep_out.at[0 : DEEP - 1], self.deep_in.at[0 : DEEP - 1], self.deep_sems.at[0],
                    self.deep_sems.at[1], self.spot.deep_peer(lax.rem(self.spot.deep + 1, DEEP)))

    def keep_own(self):
        me = self.spot.deep
        self.deep_in[me] = self.deep_out[me]

    def deep_finish(self, out_ref):
        self.keep_own()
        self.deep_whole().wait_recv()

        total = jnp.zeros((PIECE, 128), F32)
        for rank in range(DEEP):
            total = total + self.deep_in[rank].astype(F32)
        total = total * (1.0 / 512)
        lane = lax.broadcasted_iota(jnp.int32, (PIECE, 128), 1)
        share = total
        for depth in range(1, 4):
            ahead = 128 - 32 * depth
            turned = pltpu.roll(total, 128 - ahead, 1)
            moved = jnp.where(lane < 128 - ahead, turned, pltpu.roll(turned, 7, 0))
            share = jnp.where(self.spot.depth == depth, moved, share)
        out_ref[...] = share

    def drain(self):
        for part in range(len(PARTS)):
            self.pair_copy(part).wait_send()
        self.drain_plane()
        self.deep_whole().wait_send()

    def drain_plane(self):
        self.plane_whole(0, 0, DEEP).wait_send()


class FarFirst(Scatter):
    def place(self, z):
        offset = lax.rem(z - self.spot.deep + DEEP, DEEP)
        upper = lax.div(offset, 8)
        return (1 - upper) * (15 - 2 * offset) + upper * (2 * offset - 16)

    def produce(self, cols, delta):
        for step in range(3):
            rows = cols[step : step + 8].reshape(512, 9 * 128)
            self.grad[step * 1152 : (step + 1) * 1152] = lax.dot_general(
                rows, delta, (((0,), (0,)), ((), ())), preferred_element_type=F32
            )
            self.cut(*PARTS[step])
        for part in range(len(PARTS)):
            self.pair_copy(part).start()

    def merge(self):
        for part, (first, end) in enumerate(PARTS):
            self.merge_part(part)
            self.plane_start(part, first, end)

    def plane_finish(self):
        me = self.spot.plane
        self.plane_in[me] = self.merged[me]
        for part, (first, end) in enumerate(PARTS):
            self.plane_whole(part, first, end).wait_recv()
            total = jnp.zeros((end - first, PIECE, 128), F32)
            for rank in range(PLANE):
                total = total + self.plane_in[rank, first:end].astype(F32)
            self.deep_out[first:end] = total.astype(BF16)
            for place in range(first, min(end, DEEP - 1)):
                rank = lax.rem(self.spot.deep + DEEP_STEPS[place], DEEP)
                send(self.deep_out.at[place], self.deep_in.at[place], self.deep_sems.at[0], self.deep_sems.at[1],
                     self.spot.deep_peer(rank)).start()

    def keep_own(self):
        self.deep_in[DEEP - 1] = self.deep_out[DEEP - 1]

    def drain_plane(self):
        for part, (first, end) in enumerate(PARTS):
            self.plane_whole(part, first, end).wait_send()


def convolve(cols, kernel_ref):
    total = None
    for z in range(3):
        rows = cols[z : z + 8].reshape(512, 9 * 128)
        term = jnp.dot(rows, kernel_ref[z], preferred_element_type=F32)
        total = term if total is None else total + term
    return total


def turn(kernel_ref, turned):
    @pl.loop(0, 27)
    def _(k):
        turned[26 - k] = kernel_ref[k].T


def body(features, cotangent, first_hbm, second_hbm, tile_hbm, used_hbm, grad_out, first_out, second_out, *scratch):
    spot = Spot()
    scratch = list(scratch)

    def take(kind):
        count = len(kind.scratch())
        refs = scratch[:count]
        del scratch[:count]
        return kind(spot, refs)

    source_in, upstream_in, back_in = (take(Gather) for _ in range(3))
    halo_one, halo_two, halo_three, halo_four = (take(Halo) for _ in range(4))
    scatter_one, scatter_two = take(FarFirst), take(Scatter)
    news = take(News)
    (first_kernel, second_kernel, first_turned, second_turned, centre, lines, source_cols, act_cols, delta_cols, upstream,
     slope_one, slot_tile, slot_used, load_sems) = scratch

    me = spot.depth
    loads = [
        pltpu.make_async_copy(features, source_in.tiles.at[me], load_sems.at[0]),
        pltpu.make_async_copy(tile_hbm, slot_tile, load_sems.at[4]),
        pltpu.make_async_copy(used_hbm, slot_used, load_sems.at[5]),
        pltpu.make_async_copy(cotangent, upstream_in.tiles.at[me], load_sems.at[1]),
        pltpu.make_async_copy(second_hbm, second_kernel, load_sems.at[2]),
        pltpu.make_async_copy(first_hbm, first_kernel, load_sems.at[3]),
    ]
    for load in loads:
        load.start()
    greet(spot)
    loads[0].wait()
    source_in.start()
    news.tell(0)
    for load in loads[1:3]:
        load.wait()

    weights = [jnp.where(slot_tile[0, j] == me, 1.0, 0.0) * slot_used[0, j].astype(F32) for j in range(4)]
    alive = weights[0] + weights[1] + weights[2] + weights[3]
    own_tile = slot_tile[0, me]
    own_used = slot_used[0, me].astype(F32)

    def mask(condition):
        return jnp.where(condition, 1.0, 0.0)

    masks = (
        (mask(spot.depth > 0), mask(spot.depth < 3)),
        (mask(spot.deep > 0), mask(spot.deep < 15)),
        (mask(spot.column > 0), mask(spot.column < 7)),
    )
    first_taps = first_kernel.reshape(3, 1152, 128)
    second_taps = second_kernel.reshape(3, 1152, 128)
    first_back = first_turned.reshape(3, 1152, 128)
    second_back = second_turned.reshape(3, 1152, 128)

    source_in.relay()
    source_in.finish()
    halo_one.put(centre, source_in.pick(weights, slice(None)))
    halo_one.start()
    for load in loads[3:]:
        load.wait()
    upstream_in.start()
    turn(first_kernel, first_turned)
    news.hear(0)
    news.tell(1)
    halo_one.finish(centre, lines, masks, source_cols)
    act, slope = gelu_terms(convolve(source_cols, first_taps))
    slope_one[...] = slope * alive
    halo_two.put(centre, act * alive)
    halo_two.start()
    upstream_in.relay()
    news.hear(1)
    news.tell(2)
    turn(second_kernel, second_turned)
    upstream_in.finish()
    upstream[...] = upstream_in.pick(weights, slice(None))
    halo_two.finish(centre, lines, masks, act_cols)
    _, slope = gelu_terms(convolve(act_cols, second_taps))
    halo_three.put(centre, upstream[...] * slope * alive)
    halo_three.start()
    scatter_two.produce(act_cols, halo_three.tile[...].reshape(512, 128))
    news.hear(2)
    scatter_two.merge()
    halo_three.finish(centre, lines, masks, delta_cols)
    halo_four.put(centre, convolve(delta_cols, second_back) * slope_one[...])
    halo_four.start()
    scatter_one.produce(source_cols, halo_four.tile[...].reshape(512, 128))
    scatter_one.merge()
    halo_four.finish(centre, lines, masks, delta_cols)
    back_in.tiles[me] = convolve(delta_cols, first_back).astype(BF16)
    back_in.start()
    scatter_two.plane_finish()
    scatter_one.plane_finish()
    scatter_two.deep_finish(second_out)
    back_in.relay()
    back_in.finish()
    picks = [mask(own_tile == t) * own_used for t in range(4)]
    grad_out[...] = back_in.pick(picks, slice(None)).astype(BF16)
    scatter_one.deep_finish(first_out)
    for gather in (source_in, upstream_in, back_in):
        gather.drain()
    for halo in (halo_one, halo_two, halo_three, halo_four):
        halo.drain()
    scatter_two.drain()
    scatter_one.drain()


def hand_out(grad, first, second, grad_out, first_out, second_out):
    grad_out[...] = grad[...]
    for source, target in ((first, first_out), (second, second_out)):
        for row in range(6):
            target[row * 128 : (row + 1) * 128] = source[row]
        target[768:864] = source[6, :96]


def fused(features, cotangent, first_kernel, second_kernel, slot_tile, slot_used):
    whole = pl.BlockSpec(memory_space=pltpu.VMEM)
    left = pl.BlockSpec(memory_space=pl.ANY)
    piece = pltpu.VMEM((PIECE, 128), F32)
    cols = pltpu.VMEM((10, 64, 9 * 128), BF16)
    kernel = pltpu.VMEM((27, 128, 128), BF16)
    scratch = Gather.scratch() * 3 + Halo.scratch() * 4 + Scatter.scratch() * 2 + News.scratch()
    scratch += [kernel] * 4 + [pltpu.VMEM((10, 10, 8, 128), F32), pltpu.VMEM((2, 10, 16, 128), F32)] + [cols] * 3
    scratch += [pltpu.VMEM((512, 128), F32)] * 2 + [pltpu.SMEM((1, 4), jnp.int32)] * 2
    scratch += [pltpu.SemaphoreType.DMA((6,))]
    return pl.pallas_call(
        body,
        out_shape=(pltpu.VMEM((512, 128), BF16), piece, piece),
        in_specs=[left] * 6,
        out_specs=(whole, whole, whole),
        scratch_shapes=scratch,
        compiler_params=pltpu.CompilerParams(collective_id=0, has_side_effects=True, vmem_limit_bytes=56 << 20),
    )(features, cotangent, first_kernel, second_kernel, slot_tile, slot_used)


def on_device(features, cotangent, first_kernel, second_kernel, slot_tile, slot_used):
    sums = fused(
        features.reshape(512, 128), cotangent.reshape(512, 128), first_kernel, second_kernel, slot_tile, slot_used
    )
    share = jax.ShapeDtypeStruct((ROWS // 4,), F32)
    whole = pl.BlockSpec(memory_space=pltpu.VMEM)
    grad, first, second = pl.pallas_call(
        hand_out,
        out_shape=(jax.ShapeDtypeStruct((512, 128), BF16), share, share),
        in_specs=[whole] * 3,
        out_specs=(whole,) * 3,
    )(*(pltpu.with_memory_space_constraint(value, pltpu.VMEM) for value in sums))
    return (grad.reshape(features.shape), first, second)


def solution(mesh):
    tiles = P("space", "depth", None, None)
    slots = P("space", None)
    share = P(("space", "depth"))
    return jax.shard_map(
        on_device,
        mesh=mesh,
        in_specs=(tiles, tiles, P(), P(), slots, slots),
        out_specs=(tiles, share, share),
        check_vma=False,
    )
```

```python
import itertools

import jax
import jax.numpy as jnp
from jax import lax
from jax.experimental import pallas as pl
from jax.experimental.pallas import tpu as pltpu
from jax.sharding import PartitionSpec as P

MESH = pl.DeviceIdType.MESH
SLOPE_COEF = 0.7978845608028654
CUBIC_COEF = 0.044715
PLANE = 16
DEEP = 16
PIECE = 8
ROWS = 27 * 128
STEPS = [d for d in itertools.product((-1, 0, 1), repeat=3) if d != (0, 0, 0)]
PLANE_STEPS = sorted(
    [(x, y) for x in range(4) for y in range(4) if (x, y) != (0, 0)],
    key=lambda step: -min(step[0], 4 - step[0]) - min(step[1], 4 - step[1]),
)
DEEP_STEPS = (8, 7, 9, 6, 10, 5, 11, 4, 12, 3, 13, 2, 14, 1, 15)
PARTS = ((0, 5), (5, 10), (10, DEEP))
FAR_PARTS = ((0, 2), (2, 5), (5, 9), (9, DEEP))
F32 = jnp.float32
BF16 = jnp.bfloat16


def gelu_terms(values):
    inner = SLOPE_COEF * (values + CUBIC_COEF * values * values * values)
    tangent = jnp.tanh(inner)
    slope = 0.5 * (1.0 + tangent) + 0.5 * values * (1.0 - tangent * tangent) * SLOPE_COEF * (
        1.0 + 3.0 * CUBIC_COEF * values * values
    )
    return 0.5 * values * (1.0 + tangent), slope


class Spot:
    def __init__(self):
        self.space = lax.axis_index("space")
        self.depth = lax.axis_index("depth")
        self.deep = self.space // 8
        self.column = self.space % 8
        self.core = self.depth % 2
        self.x_lo = self.depth // 2
        self.plane = self.column * 2 + self.x_lo

    def plane_step(self, x, y):
        far_x = lax.rem(self.column // 4 * 2 + self.x_lo + x, 4)
        far_y = lax.rem(self.column % 4 + y, 4)
        high, low = lax.div(far_x, 2), lax.rem(far_x, 2)
        column = high * 4 + far_y
        return column * 2 + low, (self.deep * 8 + column, low * 2 + self.core)

    def deep_peer(self, rank):
        return (rank * 8 + self.column, self.depth)

    def column_peer(self, rank):
        return (self.space, rank)

    def tile_peer(self, step):
        z, x, y = step
        return (lax.rem(self.deep + x + 16, 16) * 8 + lax.rem(self.column + y + 8, 8), lax.rem(self.depth + z + 4, 4))


def greet(spot):
    barrier = pltpu.get_barrier_semaphore()

    def tell(peer):
        pl.semaphore_signal(barrier, inc=1, device_id=peer, device_id_type=MESH)

    for step in STEPS:
        tell(spot.tile_peer(step))
    for step in range(1, 4):
        tell(spot.column_peer((spot.depth + step) % 4))
    pl.semaphore_wait(barrier, len(STEPS) + 3)


class News:
    def __init__(self, spot, refs):
        self.spot = spot
        (self.sem,) = refs

    @staticmethod
    def scratch():
        return [pltpu.SemaphoreType.REGULAR((3,))]

    def peers(self, level):
        reach = 2**level
        steps = [(0, reach, 0), (0, -reach, 0), (0, 0, reach)] + ([(0, 0, -reach)] if level < 2 else [])
        return [self.spot.tile_peer(step) for step in steps]

    def tell(self, level):
        for peer in self.peers(level):
            pl.semaphore_signal(self.sem.at[level], inc=1, device_id=peer, device_id_type=MESH)

    def hear(self, level):
        pl.semaphore_wait(self.sem.at[level], len(self.peers(level)))


def send(source, target, send_sem, recv_sem, peer):
    return pltpu.make_async_remote_copy(
        src_ref=source, dst_ref=target, send_sem=send_sem, recv_sem=recv_sem, device_id=peer, device_id_type=MESH
    )


class Gather:
    def __init__(self, spot, refs):
        self.spot = spot
        self.tiles, self.sems = refs
        self.me = spot.depth
        self.pair = spot.x_lo * 2 + 1 - spot.core
        self.across = (1 - spot.x_lo) * 2 + spot.core
        self.diagonal = (1 - spot.x_lo) * 2 + 1 - spot.core

    @staticmethod
    def scratch():
        return [pltpu.VMEM((4, 512, 128), BF16), pltpu.SemaphoreType.DMA((2, 4))]

    def part(self, tile, half, way, peer, source=None):
        rows = self.tiles.at[tile] if half is None else self.tiles.at[tile, half * 256 : (half + 1) * 256]
        if source is None:
            own = rows
        else:
            own = source if half is None else source.at[half * 256 : (half + 1) * 256]
        return send(own, rows, self.sems.at[0, way], self.sems.at[1, way], self.spot.column_peer(peer))

    def start(self, source=None):
        for half in range(2):
            self.part(self.me, half, half, self.across, source).start()
        self.part(self.me, None, 2, self.pair, source).start()

    def relay(self):
        for half in range(2):
            self.part(self.across, half, half, self.across).wait_recv()
            self.part(self.across, half, 3, self.pair).start()

    def finish(self):
        self.part(self.pair, None, 2, self.pair).wait_recv()
        self.part(self.diagonal, None, 3, self.pair).wait_recv()

    def drain(self):
        for half in range(2):
            self.part(self.me, half, half, self.across).wait_send()
        self.part(self.me, None, 2, self.pair).wait_send()
        self.part(self.across, None, 3, self.pair).wait_send()

    def pick(self, weights, rows):
        total = weights[0] * self.tiles[0, rows, :].astype(F32)
        for rank in range(1, 4):
            total = total + weights[rank] * self.tiles[rank, rows, :].astype(F32)
        return total


def side(step):
    return 0 if step == 1 else 1


def last(step):
    return 7 if step == 1 else 0


class Halo:
    def __init__(self, spot, refs):
        self.spot = spot
        self.tile, self.y_face, self.xy_edge, self.inbox, self.sems = refs

    @staticmethod
    def scratch():
        shapes = [(8, 8), (2, 8), (2, 2), (68,)]
        return [pltpu.VMEM((*shape, 8, 128), BF16) for shape in shapes] + [pltpu.SemaphoreType.DMA((2,))]

    def face(self, axis, s):
        return self.inbox.at[axis * 16 + s * 8 : axis * 16 + s * 8 + 8]

    def edge(self, plane, s, r):
        return self.inbox.at[48 + plane * 4 + 2 * s + r]

    def corner(self, s, r, q):
        return self.inbox.at[60 + 4 * s + 2 * r + q]

    def ends(self, step):
        z, x, y = step
        if y == 0:
            if x == 0:
                return self.tile.at[last(z)], self.face(0, side(z))
            if z == 0:
                return self.tile.at[:, last(x)], self.face(1, side(x))
            return self.tile.at[last(z), last(x)], self.edge(0, side(z), side(x))
        if x == 0:
            if z == 0:
                return self.y_face.at[side(y)], self.face(2, side(y))
            return self.y_face.at[side(y), last(z)], self.edge(1, side(z), side(y))
        if z == 0:
            return self.xy_edge.at[side(x), side(y)], self.edge(2, side(x), side(y))
        return self.xy_edge.at[side(x), side(y)], self.corner(side(z), side(x), side(y))

    def whole(self):
        return send(self.inbox, self.inbox, self.sems.at[0], self.sems.at[1], self.spot.tile_peer((0, 0, 1)))

    def put(self, centre, values):
        rounded = values.astype(BF16).reshape(8, 8, 8, 128)
        self.tile[...] = rounded
        centre[1:9, 1:9] = rounded.astype(F32)
        flat = centre.reshape(800, 128)
        for z in range(8):
            for y in range(2):
                first = ((z + 1) * 10 + 1) * 8 + 7 - 7 * y
                self.y_face[y, z] = flat[pl.ds(first, 8, stride=8), :].astype(BF16)
        for x in range(2):
            for y in range(2):
                first = (10 + 8 - 7 * x) * 8 + 7 - 7 * y
                self.xy_edge[x, y] = flat[pl.ds(first, 8, stride=80), :].astype(BF16)

    def start(self):
        order = sorted(STEPS, key=lambda step: -abs(step[2]) * 10 - sum(abs(d) for d in step))
        for step in order:
            source, target = self.ends(step)
            send(source, target, self.sems.at[0], self.sems.at[1], self.spot.tile_peer(step)).start()

    def finish(self, centre, lines, masks, cols):
        self.whole().wait_recv()
        on_z, on_x, on_y = masks
        ends = (0, 9)
        for s in range(2):
            centre[ends[s], 1:9] = self.face(0, s)[...].astype(F32) * on_z[s]
            centre[1:9, ends[s]] = self.face(1, s)[...].astype(F32) * on_x[s]
            lines[s, 1:9, 0:8] = self.face(2, s)[...].astype(F32) * on_y[s]
            for r in range(2):
                centre[ends[s], ends[r]] = self.edge(0, s, r)[...].astype(F32) * (on_z[s] * on_x[r])
                lines[r, ends[s], 0:8] = self.edge(1, s, r)[...].astype(F32) * (on_z[s] * on_y[r])
                rows = self.edge(2, s, r)[...].astype(F32) * (on_x[s] * on_y[r])
                for z in range(8):
                    lines[r, 1 + z, 8 + s : 9 + s] = rows[z : z + 1]
                for q in range(2):
                    rows = self.corner(s, r, q)[...].astype(F32) * (on_z[s] * on_x[r] * on_y[q])
                    row = 7 - 7 * s
                    lines[q, ends[s], 8 + r : 9 + r] = rows[row : row + 1]
        row_id = lax.broadcasted_iota(jnp.int32, (8, 128), 0)

        @pl.loop(0, 10)
        def _(z):
            runs = ([], [], [])
            for x in range(10):
                place = 8 if x == 0 else 9 if x == 9 else x - 1
                middle = centre[z, x]
                low = jnp.broadcast_to(lines[0, z, place : place + 1], (8, 128))
                high = jnp.broadcast_to(lines[1, z, place : place + 1], (8, 128))
                runs[0].append(jnp.where(row_id == 0, low, pltpu.roll(middle, 1, 0)))
                runs[1].append(middle)
                runs[2].append(jnp.where(row_id == 7, high, pltpu.roll(middle, 7, 0)))
            for x in range(3):
                for y in range(3):
                    block = jnp.concatenate(runs[y][x : x + 8], axis=0).astype(BF16)
                    cols[z, :, (3 * x + y) * 128 : (3 * x + y + 1) * 128] = block

    def drain(self):
        self.whole().wait_send()


class Scatter:
    parts = PARTS

    def __init__(self, spot, refs):
        self.spot = spot
        (self.halves, self.partner, self.merged, self.plane_in, self.deep_out, self.deep_in, self.grad, self.pair_sems,
         self.plane_sems, self.deep_sems) = refs

    @staticmethod
    def scratch():
        return [
            pltpu.VMEM((2, PLANE, DEEP, PIECE, 128), BF16),
            pltpu.VMEM((PLANE, DEEP, PIECE, 128), BF16),
            pltpu.VMEM((PLANE, DEEP, PIECE, 128), BF16),
            pltpu.VMEM((PLANE, DEEP, PIECE, 128), BF16),
            pltpu.VMEM((DEEP, PIECE, 128), BF16),
            pltpu.VMEM((DEEP, PIECE, 128), BF16),
            pltpu.VMEM((ROWS, 128), F32),
            pltpu.SemaphoreType.DMA((2, 4)),
            pltpu.SemaphoreType.DMA((2, 4)),
            pltpu.SemaphoreType.DMA((2,)),
        ]

    def produce(self, cols, delta):
        for part, (first, end) in enumerate(PARTS):
            rows = cols[part : part + 8].reshape(512, 9 * 128)
            self.grad[part * 1152 : (part + 1) * 1152] = lax.dot_general(
                rows, delta, (((0,), (0,)), ((), ())), preferred_element_type=F32
            )
            self.cut(first, end)
            self.pair_copy(part).start()

    def place(self, z):
        return z

    def cut(self, first_z, end_z):

        @pl.loop(first_z, end_z)
        def _(z):
            place = self.place(z)
            rows = self.grad[pl.ds(pl.multiple_of(z * 216, 8), 216), :]
            rows = jnp.concatenate([rows, jnp.zeros((8, 128), F32)], axis=0)
            for column in range(8):
                for part in range(4):
                    first = column * 27 + part * 27 // 4
                    self.halves[part % 2, column * 2 + part // 2, place] = rows[first : first + 8].astype(BF16)

    def pair_copy(self, part):
        spot = self.spot
        other = 1 - spot.core
        first, end = self.parts[part]
        return send(self.halves.at[other, :, first:end], self.partner.at[:, first:end], self.pair_sems.at[0, part],
                    self.pair_sems.at[1, part], spot.column_peer(spot.x_lo * 2 + other))

    def merge_part(self, part):
        core = self.spot.core
        first, end = self.parts[part]
        self.pair_copy(part).wait_recv()
        for rank in range(PLANE):
            own = self.halves[core, rank, first:end].astype(F32)
            both = own + self.partner[rank, first:end].astype(F32)
            self.merged[rank, first:end] = both.astype(BF16)

    def merge(self):
        for part in range(len(self.parts)):
            self.merge_part(part)
        self.plane_start(0, 0, DEEP)

    def plane_start(self, part, first, end):
        spot = self.spot
        for x, y in PLANE_STEPS:
            rank, peer = spot.plane_step(x, y)
            send(self.merged.at[rank, first:end], self.plane_in.at[spot.plane, first:end], self.plane_sems.at[0, part],
                 self.plane_sems.at[1, part], peer).start()

    def plane_whole(self, part, first, end):
        return send(self.merged.at[0 : PLANE - 1, first:end], self.plane_in.at[0 : PLANE - 1, first:end],
                    self.plane_sems.at[0, part], self.plane_sems.at[1, part], self.spot.plane_step(1, 0)[1])

    def plane_finish(self):
        me = self.spot.plane
        self.plane_in[me] = self.merged[me]
        self.plane_whole(0, 0, DEEP).wait_recv()

        @pl.loop(0, DEEP)
        def _(z):
            total = jnp.zeros((PIECE, 128), F32)
            for rank in range(PLANE):
                total = total + self.plane_in[rank, z].astype(F32)
            self.deep_out[z] = total.astype(BF16)

        for step in DEEP_STEPS:
            rank = lax.rem(self.spot.deep + step, DEEP)
            send(self.deep_out.at[rank], self.deep_in.at[self.spot.deep], self.deep_sems.at[0], self.deep_sems.at[1],
                 self.spot.deep_peer(rank)).start()

    def deep_whole(self):
        return send(self.deep_out.at[0 : DEEP - 1], self.deep_in.at[0 : DEEP - 1], self.deep_sems.at[0],
                    self.deep_sems.at[1], self.spot.deep_peer(lax.rem(self.spot.deep + 1, DEEP)))

    def keep_own(self):
        me = self.spot.deep
        self.deep_in[me] = self.deep_out[me]

    def deep_finish(self, out_ref):
        self.keep_own()
        self.deep_whole().wait_recv()

        total = jnp.zeros((PIECE, 128), F32)
        for rank in range(DEEP):
            total = total + self.deep_in[rank].astype(F32)
        total = total * (1.0 / 512)
        lane = lax.broadcasted_iota(jnp.int32, (PIECE, 128), 1)
        share = total
        for depth in range(1, 4):
            ahead = 128 - 32 * depth
            turned = pltpu.roll(total, 128 - ahead, 1)
            moved = jnp.where(lane < 128 - ahead, turned, pltpu.roll(turned, 7, 0))
            share = jnp.where(self.spot.depth == depth, moved, share)
        out_ref[...] = share

    def drain(self):
        for part in range(len(self.parts)):
            self.pair_copy(part).wait_send()
        self.drain_plane()
        self.deep_whole().wait_send()

    def drain_plane(self):
        self.plane_whole(0, 0, DEEP).wait_send()


class FarFirst(Scatter):
    parts = FAR_PARTS

    def place(self, z):
        offset = lax.rem(z - self.spot.deep + DEEP, DEEP)
        upper = lax.div(offset, 8)
        return (1 - upper) * (15 - 2 * offset) + upper * (2 * offset - 16)

    def produce(self, cols, delta):
        for step in range(3):
            rows = cols[step : step + 8].reshape(512, 9 * 128)
            self.grad[step * 1152 : (step + 1) * 1152] = lax.dot_general(
                rows, delta, (((0,), (0,)), ((), ())), preferred_element_type=F32
            )
            self.cut(*PARTS[step])
        for part in range(len(self.parts)):
            self.pair_copy(part).start()

    def merge(self):
        for part, (first, end) in enumerate(self.parts):
            self.merge_part(part)
            self.plane_start(part, first, end)

    def plane_finish(self):
        me = self.spot.plane
        self.plane_in[me] = self.merged[me]
        for part, (first, end) in enumerate(self.parts):
            self.plane_whole(part, first, end).wait_recv()
            total = jnp.zeros((end - first, PIECE, 128), F32)
            for rank in range(PLANE):
                total = total + self.plane_in[rank, first:end].astype(F32)
            self.deep_out[first:end] = total.astype(BF16)
            for place in range(first, min(end, DEEP - 1)):
                rank = lax.rem(self.spot.deep + DEEP_STEPS[place], DEEP)
                send(self.deep_out.at[place], self.deep_in.at[place], self.deep_sems.at[0], self.deep_sems.at[1],
                     self.spot.deep_peer(rank)).start()

    def keep_own(self):
        self.deep_in[DEEP - 1] = self.deep_out[DEEP - 1]

    def drain_plane(self):
        for part, (first, end) in enumerate(self.parts):
            self.plane_whole(part, first, end).wait_send()


def convolve(cols, kernel_ref):
    total = None
    for z in range(3):
        rows = cols[z : z + 8].reshape(512, 9 * 128)
        term = jnp.dot(rows, kernel_ref[z], preferred_element_type=F32)
        total = term if total is None else total + term
    return total


def turn(kernel_ref, turned):
    @pl.loop(0, 27)
    def _(k):
        turned[26 - k] = kernel_ref[k].T


def body(features, cotangent, first_hbm, second_hbm, tile_hbm, used_hbm, grad_out, first_out, second_out, *scratch):
    spot = Spot()
    scratch = list(scratch)

    def take(kind):
        count = len(kind.scratch())
        refs = scratch[:count]
        del scratch[:count]
        return kind(spot, refs)

    source_in, upstream_in, back_in = (take(Gather) for _ in range(3))
    halo_one, halo_two, halo_three, halo_four = (take(Halo) for _ in range(4))
    scatter_one, scatter_two = take(FarFirst), take(Scatter)
    news = take(News)
    (first_kernel, second_kernel, first_turned, second_turned, centre, lines, source_cols, act_cols, delta_cols, upstream,
     slope_one, slot_tile, slot_used, load_sems) = scratch

    me = spot.depth
    loads = [
        pltpu.make_async_copy(features, source_in.tiles.at[me], load_sems.at[0]),
        pltpu.make_async_copy(tile_hbm, slot_tile, load_sems.at[4]),
        pltpu.make_async_copy(used_hbm, slot_used, load_sems.at[5]),
        pltpu.make_async_copy(cotangent, upstream_in.tiles.at[me], load_sems.at[1]),
        pltpu.make_async_copy(second_hbm, second_kernel, load_sems.at[2]),
        pltpu.make_async_copy(first_hbm, first_kernel, load_sems.at[3]),
    ]
    for load in loads:
        load.start()
    greet(spot)
    source_in.start(features)
    news.tell(0)
    for load in loads[:3]:
        load.wait()

    weights = [jnp.where(slot_tile[0, j] == me, 1.0, 0.0) * slot_used[0, j].astype(F32) for j in range(4)]
    alive = weights[0] + weights[1] + weights[2] + weights[3]
    own_tile = slot_tile[0, me]
    own_used = slot_used[0, me].astype(F32)

    def mask(condition):
        return jnp.where(condition, 1.0, 0.0)

    masks = (
        (mask(spot.depth > 0), mask(spot.depth < 3)),
        (mask(spot.deep > 0), mask(spot.deep < 15)),
        (mask(spot.column > 0), mask(spot.column < 7)),
    )
    first_taps = first_kernel.reshape(3, 1152, 128)
    second_taps = second_kernel.reshape(3, 1152, 128)
    first_back = first_turned.reshape(3, 1152, 128)
    second_back = second_turned.reshape(3, 1152, 128)

    source_in.relay()
    source_in.finish()
    halo_one.put(centre, source_in.pick(weights, slice(None)))
    halo_one.start()
    for load in loads[3:]:
        load.wait()
    upstream_in.start(cotangent)
    turn(first_kernel, first_turned)
    news.hear(0)
    news.tell(1)
    halo_one.finish(centre, lines, masks, source_cols)
    act, slope = gelu_terms(convolve(source_cols, first_taps))
    slope_one[...] = slope * alive
    halo_two.put(centre, act * alive)
    halo_two.start()
    upstream_in.relay()
    news.hear(1)
    news.tell(2)
    turn(second_kernel, second_turned)
    upstream_in.finish()
    upstream[...] = upstream_in.pick(weights, slice(None))
    halo_two.finish(centre, lines, masks, act_cols)
    _, slope = gelu_terms(convolve(act_cols, second_taps))
    halo_three.put(centre, upstream[...] * slope * alive)
    halo_three.start()
    scatter_two.produce(act_cols, halo_three.tile[...].reshape(512, 128))
    news.hear(2)
    scatter_two.merge()
    halo_three.finish(centre, lines, masks, delta_cols)
    halo_four.put(centre, convolve(delta_cols, second_back) * slope_one[...])
    halo_four.start()
    scatter_one.produce(source_cols, halo_four.tile[...].reshape(512, 128))
    scatter_one.merge()
    halo_four.finish(centre, lines, masks, delta_cols)
    back_in.tiles[me] = convolve(delta_cols, first_back).astype(BF16)
    back_in.start()
    scatter_two.plane_finish()
    scatter_one.plane_finish()
    scatter_two.deep_finish(second_out)
    back_in.relay()
    back_in.finish()
    picks = [mask(own_tile == t) * own_used for t in range(4)]
    grad_out[...] = back_in.pick(picks, slice(None)).astype(BF16)
    scatter_one.deep_finish(first_out)
    for gather in (source_in, upstream_in, back_in):
        gather.drain()
    for halo in (halo_one, halo_two, halo_three, halo_four):
        halo.drain()
    scatter_two.drain()
    scatter_one.drain()


def hand_out(grad, first, second, grad_out, first_out, second_out):
    grad_out[...] = grad[...]
    for source, target in ((first, first_out), (second, second_out)):
        for row in range(6):
            target[row * 128 : (row + 1) * 128] = source[row]
        target[768:864] = source[6, :96]


def fused(features, cotangent, first_kernel, second_kernel, slot_tile, slot_used):
    whole = pl.BlockSpec(memory_space=pltpu.VMEM)
    left = pl.BlockSpec(memory_space=pl.ANY)
    piece = pltpu.VMEM((PIECE, 128), F32)
    cols = pltpu.VMEM((10, 64, 9 * 128), BF16)
    kernel = pltpu.VMEM((27, 128, 128), BF16)
    scratch = Gather.scratch() * 3 + Halo.scratch() * 4 + Scatter.scratch() * 2 + News.scratch()
    scratch += [kernel] * 4 + [pltpu.VMEM((10, 10, 8, 128), F32), pltpu.VMEM((2, 10, 16, 128), F32)] + [cols] * 3
    scratch += [pltpu.VMEM((512, 128), F32)] * 2 + [pltpu.SMEM((1, 4), jnp.int32)] * 2
    scratch += [pltpu.SemaphoreType.DMA((6,))]
    return pl.pallas_call(
        body,
        out_shape=(pltpu.VMEM((512, 128), BF16), piece, piece),
        in_specs=[left] * 6,
        out_specs=(whole, whole, whole),
        scratch_shapes=scratch,
        compiler_params=pltpu.CompilerParams(collective_id=0, has_side_effects=True, vmem_limit_bytes=56 << 20),
    )(features, cotangent, first_kernel, second_kernel, slot_tile, slot_used)


def on_device(features, cotangent, first_kernel, second_kernel, slot_tile, slot_used):
    sums = fused(
        features.reshape(512, 128), cotangent.reshape(512, 128), first_kernel, second_kernel, slot_tile, slot_used
    )
    share = jax.ShapeDtypeStruct((ROWS // 4,), F32)
    whole = pl.BlockSpec(memory_space=pltpu.VMEM)
    grad, first, second = pl.pallas_call(
        hand_out,
        out_shape=(jax.ShapeDtypeStruct((512, 128), BF16), share, share),
        in_specs=[whole] * 3,
        out_specs=(whole,) * 3,
    )(*(pltpu.with_memory_space_constraint(value, pltpu.VMEM) for value in sums))
    return (grad.reshape(features.shape), first, second)


def solution(mesh):
    tiles = P("space", "depth", None, None)
    slots = P("space", None)
    share = P(("space", "depth"))
    return jax.shard_map(
        on_device,
        mesh=mesh,
        in_specs=(tiles, tiles, P(), P(), slots, slots),
        out_specs=(tiles, share, share),
        check_vma=False,
    )
```

```python
import itertools

import jax
import jax.numpy as jnp
from jax import lax
from jax.experimental import pallas as pl
from jax.experimental.pallas import tpu as pltpu
from jax.sharding import PartitionSpec as P

MESH = pl.DeviceIdType.MESH
SLOPE_COEF = 0.7978845608028654
CUBIC_COEF = 0.044715
PLANE = 16
DEEP = 16
PIECE = 8
ROWS = 27 * 128
STEPS = [d for d in itertools.product((-1, 0, 1), repeat=3) if d != (0, 0, 0)]
PLANE_STEPS = sorted(
    [(x, y) for x in range(4) for y in range(4) if (x, y) != (0, 0)],
    key=lambda step: -min(step[0], 4 - step[0]) - min(step[1], 4 - step[1]),
)
DEEP_STEPS = (8, 7, 9, 6, 10, 5, 11, 4, 12, 3, 13, 2, 14, 1, 15)
PARTS = ((0, 5), (5, 10), (10, DEEP))
F32 = jnp.float32
BF16 = jnp.bfloat16


def gelu_terms(values):
    inner = SLOPE_COEF * (values + CUBIC_COEF * values * values * values)
    tangent = jnp.tanh(inner)
    slope = 0.5 * (1.0 + tangent) + 0.5 * values * (1.0 - tangent * tangent) * SLOPE_COEF * (
        1.0 + 3.0 * CUBIC_COEF * values * values
    )
    return 0.5 * values * (1.0 + tangent), slope


class Spot:
    def __init__(self):
        self.space = lax.axis_index("space")
        self.depth = lax.axis_index("depth")
        self.deep = self.space // 8
        self.column = self.space % 8
        self.core = self.depth % 2
        self.x_lo = self.depth // 2
        self.plane = self.column * 2 + self.x_lo

    def plane_step(self, x, y):
        far_x = lax.rem(self.column // 4 * 2 + self.x_lo + x, 4)
        far_y = lax.rem(self.column % 4 + y, 4)
        high, low = lax.div(far_x, 2), lax.rem(far_x, 2)
        column = high * 4 + far_y
        return column * 2 + low, (self.deep * 8 + column, low * 2 + self.core)

    def deep_peer(self, rank):
        return (rank * 8 + self.column, self.depth)

    def column_peer(self, rank):
        return (self.space, rank)

    def tile_peer(self, step):
        z, x, y = step
        return (lax.rem(self.deep + x + 16, 16) * 8 + lax.rem(self.column + y + 8, 8), lax.rem(self.depth + z + 4, 4))


def greet(spot):
    barrier = pltpu.get_barrier_semaphore()

    def tell(peer):
        pl.semaphore_signal(barrier, inc=1, device_id=peer, device_id_type=MESH)

    for step in STEPS:
        tell(spot.tile_peer(step))
    for step in range(1, 4):
        tell(spot.column_peer((spot.depth + step) % 4))
    pl.semaphore_wait(barrier, len(STEPS) + 3)


class News:
    def __init__(self, spot, refs):
        self.spot = spot
        (self.sem,) = refs

    @staticmethod
    def scratch():
        return [pltpu.SemaphoreType.REGULAR((3,))]

    def peers(self, level):
        reach = 2**level
        steps = [(0, reach, 0), (0, -reach, 0), (0, 0, reach)] + ([(0, 0, -reach)] if level < 2 else [])
        return [self.spot.tile_peer(step) for step in steps]

    def tell(self, level):
        for peer in self.peers(level):
            pl.semaphore_signal(self.sem.at[level], inc=1, device_id=peer, device_id_type=MESH)

    def hear(self, level):
        pl.semaphore_wait(self.sem.at[level], len(self.peers(level)))


def send(source, target, send_sem, recv_sem, peer):
    return pltpu.make_async_remote_copy(
        src_ref=source, dst_ref=target, send_sem=send_sem, recv_sem=recv_sem, device_id=peer, device_id_type=MESH
    )


class Gather:
    def __init__(self, spot, refs):
        self.spot = spot
        self.tiles, self.sems = refs
        self.me = spot.depth
        self.pair = spot.x_lo * 2 + 1 - spot.core
        self.across = (1 - spot.x_lo) * 2 + spot.core
        self.diagonal = (1 - spot.x_lo) * 2 + 1 - spot.core

    @staticmethod
    def scratch():
        return [pltpu.VMEM((4, 512, 128), BF16), pltpu.SemaphoreType.DMA((2, 4))]

    def part(self, tile, half, way, peer):
        rows = self.tiles.at[tile] if half is None else self.tiles.at[tile, half * 256 : (half + 1) * 256]
        return send(rows, rows, self.sems.at[0, way], self.sems.at[1, way], self.spot.column_peer(peer))

    def start(self):
        for half in range(2):
            self.part(self.me, half, half, self.across).start()
        self.part(self.me, None, 2, self.pair).start()

    def relay(self):
        for half in range(2):
            self.part(self.across, half, half, self.across).wait_recv()
            self.part(self.across, half, 3, self.pair).start()

    def finish(self):
        self.part(self.pair, None, 2, self.pair).wait_recv()
        self.part(self.diagonal, None, 3, self.pair).wait_recv()

    def drain(self):
        for half in range(2):
            self.part(self.me, half, half, self.across).wait_send()
        self.part(self.me, None, 2, self.pair).wait_send()
        self.part(self.across, None, 3, self.pair).wait_send()

    def pick(self, weights, rows):
        total = weights[0] * self.tiles[0, rows, :].astype(F32)
        for rank in range(1, 4):
            total = total + weights[rank] * self.tiles[rank, rows, :].astype(F32)
        return total


def side(step):
    return 0 if step == 1 else 1


def last(step):
    return 7 if step == 1 else 0


class Halo:
    def __init__(self, spot, refs):
        self.spot = spot
        self.tile, self.y_face, self.xy_edge, self.inbox, self.sems = refs

    @staticmethod
    def scratch():
        shapes = [(8, 8), (2, 8), (2, 2), (68,)]
        return [pltpu.VMEM((*shape, 8, 128), BF16) for shape in shapes] + [pltpu.SemaphoreType.DMA((2,))]

    def face(self, axis, s):
        return self.inbox.at[axis * 16 + s * 8 : axis * 16 + s * 8 + 8]

    def edge(self, plane, s, r):
        return self.inbox.at[48 + plane * 4 + 2 * s + r]

    def corner(self, s, r, q):
        return self.inbox.at[60 + 4 * s + 2 * r + q]

    def ends(self, step):
        z, x, y = step
        if y == 0:
            if x == 0:
                return self.tile.at[last(z)], self.face(0, side(z))
            if z == 0:
                return self.tile.at[:, last(x)], self.face(1, side(x))
            return self.tile.at[last(z), last(x)], self.edge(0, side(z), side(x))
        if x == 0:
            if z == 0:
                return self.y_face.at[side(y)], self.face(2, side(y))
            return self.y_face.at[side(y), last(z)], self.edge(1, side(z), side(y))
        if z == 0:
            return self.xy_edge.at[side(x), side(y)], self.edge(2, side(x), side(y))
        return self.xy_edge.at[side(x), side(y)], self.corner(side(z), side(x), side(y))

    def whole(self):
        return send(self.inbox, self.inbox, self.sems.at[0], self.sems.at[1], self.spot.tile_peer((0, 0, 1)))

    def put(self, centre, values):
        rounded = values.astype(BF16).reshape(8, 8, 8, 128)
        self.tile[...] = rounded
        centre[1:9, 1:9] = rounded.astype(F32)
        flat = centre.reshape(800, 128)
        for z in range(8):
            for y in range(2):
                first = ((z + 1) * 10 + 1) * 8 + 7 - 7 * y
                self.y_face[y, z] = flat[pl.ds(first, 8, stride=8), :].astype(BF16)
        for x in range(2):
            for y in range(2):
                first = (10 + 8 - 7 * x) * 8 + 7 - 7 * y
                self.xy_edge[x, y] = flat[pl.ds(first, 8, stride=80), :].astype(BF16)

    def start(self):
        order = sorted(STEPS, key=lambda step: -abs(step[2]) * 10 - sum(abs(d) for d in step))
        for step in order:
            source, target = self.ends(step)
            send(source, target, self.sems.at[0], self.sems.at[1], self.spot.tile_peer(step)).start()

    def finish(self, centre, lines, masks, cols):
        self.whole().wait_recv()
        on_z, on_x, on_y = masks
        ends = (0, 9)
        for s in range(2):
            centre[ends[s], 1:9] = self.face(0, s)[...].astype(F32) * on_z[s]
            centre[1:9, ends[s]] = self.face(1, s)[...].astype(F32) * on_x[s]
            lines[s, 1:9, 0:8] = self.face(2, s)[...].astype(F32) * on_y[s]
            for r in range(2):
                centre[ends[s], ends[r]] = self.edge(0, s, r)[...].astype(F32) * (on_z[s] * on_x[r])
                lines[r, ends[s], 0:8] = self.edge(1, s, r)[...].astype(F32) * (on_z[s] * on_y[r])
                rows = self.edge(2, s, r)[...].astype(F32) * (on_x[s] * on_y[r])
                for z in range(8):
                    lines[r, 1 + z, 8 + s : 9 + s] = rows[z : z + 1]
                for q in range(2):
                    rows = self.corner(s, r, q)[...].astype(F32) * (on_z[s] * on_x[r] * on_y[q])
                    row = 7 - 7 * s
                    lines[q, ends[s], 8 + r : 9 + r] = rows[row : row + 1]
        row_id = lax.broadcasted_iota(jnp.int32, (8, 128), 0)

        @pl.loop(0, 10)
        def _(z):
            runs = ([], [], [])
            for x in range(10):
                place = 8 if x == 0 else 9 if x == 9 else x - 1
                middle = centre[z, x]
                low = jnp.broadcast_to(lines[0, z, place : place + 1], (8, 128))
                high = jnp.broadcast_to(lines[1, z, place : place + 1], (8, 128))
                runs[0].append(jnp.where(row_id == 0, low, pltpu.roll(middle, 1, 0)))
                runs[1].append(middle)
                runs[2].append(jnp.where(row_id == 7, high, pltpu.roll(middle, 7, 0)))
            for x in range(3):
                for y in range(3):
                    block = jnp.concatenate(runs[y][x : x + 8], axis=0).astype(BF16)
                    cols[z, :, (3 * x + y) * 128 : (3 * x + y + 1) * 128] = block

    def drain(self):
        self.whole().wait_send()


class Scatter:
    def __init__(self, spot, refs):
        self.spot = spot
        (self.halves, self.partner, self.merged, self.plane_in, self.deep_out, self.deep_in, self.grad, self.pair_sems,
         self.plane_sems, self.deep_sems) = refs

    @staticmethod
    def scratch():
        return [
            pltpu.VMEM((2, PLANE, DEEP, PIECE, 128), BF16),
            pltpu.VMEM((PLANE, DEEP, PIECE, 128), BF16),
            pltpu.VMEM((PLANE, DEEP, PIECE, 128), BF16),
            pltpu.VMEM((PLANE, DEEP, PIECE, 128), BF16),
            pltpu.VMEM((DEEP, PIECE, 128), BF16),
            pltpu.VMEM((DEEP, PIECE, 128), BF16),
            pltpu.VMEM((ROWS + 8, 128), F32),
            pltpu.SemaphoreType.DMA((2, len(PARTS))),
            pltpu.SemaphoreType.DMA((2, len(PARTS))),
            pltpu.SemaphoreType.DMA((2,)),
        ]

    def produce(self, cols, delta):
        for part, (first, end) in enumerate(PARTS):
            rows = cols[part : part + 8].reshape(512, 9 * 128)
            self.grad[part * 1152 : (part + 1) * 1152] = lax.dot_general(
                rows, delta, (((0,), (0,)), ((), ())), preferred_element_type=F32
            )
            self.cut(first, end)
            self.pair_copy(part).start()

    def place(self, z):
        return z

    def cut(self, first_z, end_z):

        @pl.loop(first_z, end_z)
        def _(z):
            place = self.place(z)
            for column in range(8):
                for part in range(4):
                    first = column * 27 + part * 27 // 4
                    self.halves[part % 2, column * 2 + part // 2, place] = self.grad[pl.ds(z * 216 + first, 8), :].astype(BF16)

    def pair_copy(self, part):
        spot = self.spot
        other = 1 - spot.core
        first, end = PARTS[part]
        return send(self.halves.at[other, :, first:end], self.partner.at[:, first:end], self.pair_sems.at[0, part],
                    self.pair_sems.at[1, part], spot.column_peer(spot.x_lo * 2 + other))

    def merge_part(self, part):
        core = self.spot.core
        first, end = PARTS[part]
        self.pair_copy(part).wait_recv()
        for rank in range(PLANE):
            own = self.halves[core, rank, first:end].astype(F32)
            both = own + self.partner[rank, first:end].astype(F32)
            self.merged[rank, first:end] = both.astype(BF16)

    def merge(self):
        for part in range(len(PARTS)):
            self.merge_part(part)
        self.plane_start(0, 0, DEEP)

    def plane_start(self, part, first, end):
        spot = self.spot
        for x, y in PLANE_STEPS:
            rank, peer = spot.plane_step(x, y)
            send(self.merged.at[rank, first:end], self.plane_in.at[spot.plane, first:end], self.plane_sems.at[0, part],
                 self.plane_sems.at[1, part], peer).start()

    def plane_whole(self, part, first, end):
        return send(self.merged.at[0 : PLANE - 1, first:end], self.plane_in.at[0 : PLANE - 1, first:end],
                    self.plane_sems.at[0, part], self.plane_sems.at[1, part], self.spot.plane_step(1, 0)[1])

    def plane_finish(self):
        me = self.spot.plane
        self.plane_in[me] = self.merged[me]
        self.plane_whole(0, 0, DEEP).wait_recv()

        @pl.loop(0, DEEP)
        def _(z):
            total = jnp.zeros((PIECE, 128), F32)
            for rank in range(PLANE):
                total = total + self.plane_in[rank, z].astype(F32)
            self.deep_out[z] = total.astype(BF16)

        for step in DEEP_STEPS:
            rank = lax.rem(self.spot.deep + step, DEEP)
            send(self.deep_out.at[rank], self.deep_in.at[self.spot.deep], self.deep_sems.at[0], self.deep_sems.at[1],
                 self.spot.deep_peer(rank)).start()

    def deep_whole(self):
        return send(self.deep_out.at[0 : DEEP - 1], self.deep_in.at[0 : DEEP - 1], self.deep_sems.at[0],
                    self.deep_sems.at[1], self.spot.deep_peer(lax.rem(self.spot.deep + 1, DEEP)))

    def keep_own(self):
        me = self.spot.deep
        self.deep_in[me] = self.deep_out[me]

    def deep_finish(self, out_ref):
        self.keep_own()
        self.deep_whole().wait_recv()

        total = jnp.zeros((PIECE, 128), F32)
        for rank in range(DEEP):
            total = total + self.deep_in[rank].astype(F32)
        total = total * (1.0 / 512)
        lane = lax.broadcasted_iota(jnp.int32, (PIECE, 128), 1)
        share = total
        for depth in range(1, 4):
            ahead = 128 - 32 * depth
            turned = pltpu.roll(total, 128 - ahead, 1)
            moved = jnp.where(lane < 128 - ahead, turned, pltpu.roll(turned, 7, 0))
            share = jnp.where(self.spot.depth == depth, moved, share)
        out_ref[...] = share

    def drain(self):
        for part in range(len(PARTS)):
            self.pair_copy(part).wait_send()
        self.drain_plane()
        self.deep_whole().wait_send()

    def drain_plane(self):
        self.plane_whole(0, 0, DEEP).wait_send()


class FarFirst(Scatter):
    def place(self, z):
        offset = lax.rem(z - self.spot.deep + DEEP, DEEP)
        upper = lax.div(offset, 8)
        return (1 - upper) * (15 - 2 * offset) + upper * (2 * offset - 16)

    def produce(self, cols, delta):
        for step in range(3):
            rows = cols[step : step + 8].reshape(512, 9 * 128)
            self.grad[step * 1152 : (step + 1) * 1152] = lax.dot_general(
                rows, delta, (((0,), (0,)), ((), ())), preferred_element_type=F32
            )
            self.cut(*PARTS[step])
        for part in range(len(PARTS)):
            self.pair_copy(part).start()

    def merge(self):
        for part, (first, end) in enumerate(PARTS):
            self.merge_part(part)
            self.plane_start(part, first, end)

    def plane_finish(self):
        me = self.spot.plane
        self.plane_in[me] = self.merged[me]
        for part, (first, end) in enumerate(PARTS):
            self.plane_whole(part, first, end).wait_recv()
            total = jnp.zeros((end - first, PIECE, 128), F32)
            for rank in range(PLANE):
                total = total + self.plane_in[rank, first:end].astype(F32)
            self.deep_out[first:end] = total.astype(BF16)
            for place in range(first, min(end, DEEP - 1)):
                rank = lax.rem(self.spot.deep + DEEP_STEPS[place], DEEP)
                send(self.deep_out.at[place], self.deep_in.at[place], self.deep_sems.at[0], self.deep_sems.at[1],
                     self.spot.deep_peer(rank)).start()

    def keep_own(self):
        self.deep_in[DEEP - 1] = self.deep_out[DEEP - 1]

    def drain_plane(self):
        for part, (first, end) in enumerate(PARTS):
            self.plane_whole(part, first, end).wait_send()


def convolve(cols, kernel_ref):
    total = None
    for z in range(3):
        rows = cols[z : z + 8].reshape(512, 9 * 128)
        term = jnp.dot(rows, kernel_ref[z], preferred_element_type=F32)
        total = term if total is None else total + term
    return total


def turn(kernel_ref, turned):
    @pl.loop(0, 27)
    def _(k):
        turned[26 - k] = kernel_ref[k].T


def body(features, cotangent, first_hbm, second_hbm, tile_hbm, used_hbm, grad_out, first_out, second_out, *scratch):
    spot = Spot()
    scratch = list(scratch)

    def take(kind):
        count = len(kind.scratch())
        refs = scratch[:count]
        del scratch[:count]
        return kind(spot, refs)

    source_in, upstream_in, back_in = (take(Gather) for _ in range(3))
    halo_one, halo_two, halo_three, halo_four = (take(Halo) for _ in range(4))
    scatter_one, scatter_two = take(FarFirst), take(Scatter)
    news = take(News)
    (first_kernel, second_kernel, first_turned, second_turned, centre, lines, source_cols, act_cols, delta_cols, upstream,
     slope_one, slot_tile, slot_used, load_sems) = scratch

    me = spot.depth
    loads = [
        pltpu.make_async_copy(features, source_in.tiles.at[me], load_sems.at[0]),
        pltpu.make_async_copy(tile_hbm, slot_tile, load_sems.at[4]),
        pltpu.make_async_copy(used_hbm, slot_used, load_sems.at[5]),
        pltpu.make_async_copy(cotangent, upstream_in.tiles.at[me], load_sems.at[1]),
        pltpu.make_async_copy(second_hbm, second_kernel, load_sems.at[2]),
        pltpu.make_async_copy(first_hbm, first_kernel, load_sems.at[3]),
    ]
    for load in loads:
        load.start()
    greet(spot)
    loads[0].wait()
    source_in.start()
    news.tell(0)
    for load in loads[1:3]:
        load.wait()

    weights = [jnp.where(slot_tile[0, j] == me, 1.0, 0.0) * slot_used[0, j].astype(F32) for j in range(4)]
    alive = weights[0] + weights[1] + weights[2] + weights[3]
    own_tile = slot_tile[0, me]
    own_used = slot_used[0, me].astype(F32)

    def mask(condition):
        return jnp.where(condition, 1.0, 0.0)

    masks = (
        (mask(spot.depth > 0), mask(spot.depth < 3)),
        (mask(spot.deep > 0), mask(spot.deep < 15)),
        (mask(spot.column > 0), mask(spot.column < 7)),
    )
    first_taps = first_kernel.reshape(3, 1152, 128)
    second_taps = second_kernel.reshape(3, 1152, 128)
    first_back = first_turned.reshape(3, 1152, 128)
    second_back = second_turned.reshape(3, 1152, 128)

    source_in.relay()
    source_in.finish()
    halo_one.put(centre, source_in.pick(weights, slice(None)))
    halo_one.start()
    for load in loads[3:]:
        load.wait()
    upstream_in.start()
    turn(first_kernel, first_turned)
    for scatter in (scatter_one, scatter_two):
        scatter.grad[ROWS : ROWS + 8] = jnp.zeros((8, 128), F32)
    news.hear(0)
    news.tell(1)
    halo_one.finish(centre, lines, masks, source_cols)
    act, slope = gelu_terms(convolve(source_cols, first_taps))
    slope_one[...] = slope * alive
    halo_two.put(centre, act * alive)
    halo_two.start()
    upstream_in.relay()
    news.hear(1)
    news.tell(2)
    turn(second_kernel, second_turned)
    upstream_in.finish()
    upstream[...] = upstream_in.pick(weights, slice(None))
    halo_two.finish(centre, lines, masks, act_cols)
    _, slope = gelu_terms(convolve(act_cols, second_taps))
    halo_three.put(centre, upstream[...] * slope * alive)
    halo_three.start()
    scatter_two.produce(act_cols, halo_three.tile[...].reshape(512, 128))
    news.hear(2)
    scatter_two.merge()
    halo_three.finish(centre, lines, masks, delta_cols)
    halo_four.put(centre, convolve(delta_cols, second_back) * slope_one[...])
    halo_four.start()
    scatter_one.produce(source_cols, halo_four.tile[...].reshape(512, 128))
    scatter_one.merge()
    halo_four.finish(centre, lines, masks, delta_cols)
    back_in.tiles[me] = convolve(delta_cols, first_back).astype(BF16)
    back_in.start()
    scatter_two.plane_finish()
    scatter_one.plane_finish()
    scatter_two.deep_finish(second_out)
    back_in.relay()
    back_in.finish()
    picks = [mask(own_tile == t) * own_used for t in range(4)]
    grad_out[...] = back_in.pick(picks, slice(None)).astype(BF16)
    scatter_one.deep_finish(first_out)
    for gather in (source_in, upstream_in, back_in):
        gather.drain()
    for halo in (halo_one, halo_two, halo_three, halo_four):
        halo.drain()
    scatter_two.drain()
    scatter_one.drain()


def hand_out(grad, first, second, grad_out, first_out, second_out):
    grad_out[...] = grad[...]
    for source, target in ((first, first_out), (second, second_out)):
        for row in range(6):
            target[row * 128 : (row + 1) * 128] = source[row]
        target[768:864] = source[6, :96]


def fused(features, cotangent, first_kernel, second_kernel, slot_tile, slot_used):
    whole = pl.BlockSpec(memory_space=pltpu.VMEM)
    left = pl.BlockSpec(memory_space=pl.ANY)
    piece = pltpu.VMEM((PIECE, 128), F32)
    cols = pltpu.VMEM((10, 64, 9 * 128), BF16)
    kernel = pltpu.VMEM((27, 128, 128), BF16)
    scratch = Gather.scratch() * 3 + Halo.scratch() * 4 + Scatter.scratch() * 2 + News.scratch()
    scratch += [kernel] * 4 + [pltpu.VMEM((10, 10, 8, 128), F32), pltpu.VMEM((2, 10, 16, 128), F32)] + [cols] * 3
    scratch += [pltpu.VMEM((512, 128), F32)] * 2 + [pltpu.SMEM((1, 4), jnp.int32)] * 2
    scratch += [pltpu.SemaphoreType.DMA((6,))]
    return pl.pallas_call(
        body,
        out_shape=(pltpu.VMEM((512, 128), BF16), piece, piece),
        in_specs=[left] * 6,
        out_specs=(whole, whole, whole),
        scratch_shapes=scratch,
        compiler_params=pltpu.CompilerParams(collective_id=0, has_side_effects=True, vmem_limit_bytes=56 << 20),
    )(features, cotangent, first_kernel, second_kernel, slot_tile, slot_used)


def on_device(features, cotangent, first_kernel, second_kernel, slot_tile, slot_used):
    sums = fused(
        features.reshape(512, 128), cotangent.reshape(512, 128), first_kernel, second_kernel, slot_tile, slot_used
    )
    share = jax.ShapeDtypeStruct((ROWS // 4,), F32)
    whole = pl.BlockSpec(memory_space=pltpu.VMEM)
    grad, first, second = pl.pallas_call(
        hand_out,
        out_shape=(jax.ShapeDtypeStruct((512, 128), BF16), share, share),
        in_specs=[whole] * 3,
        out_specs=(whole,) * 3,
    )(*(pltpu.with_memory_space_constraint(value, pltpu.VMEM) for value in sums))
    return (grad.reshape(features.shape), first, second)


def solution(mesh):
    tiles = P("space", "depth", None, None)
    slots = P("space", None)
    share = P(("space", "depth"))
    return jax.shard_map(
        on_device,
        mesh=mesh,
        in_specs=(tiles, tiles, P(), P(), slots, slots),
        out_specs=(tiles, share, share),
        check_vma=False,
    )
```
